512 devices in a mesh: ctx: 16 (over z, x_hi), head: 32 (over y, x_lo, core).
Axes of the slice: x: 4 (x_hi: 2, x_lo: 2; x = x_hi * 2 + x_lo), y: 8, z: 8, core: 2. Of those that a mesh axis runs over, the one named last changes fastest.
Arguments:
- x_in: bfloat16 [4096, 16384], P('ctx', 'head'), may hold values from -64 to 64
- z_in: bfloat16 [4096, 16384], P('ctx', 'head'), may hold values from -6 to 6
- bc_in: bfloat16 [4096, 2048], P('ctx'), may hold values from -0.8984375 to 0.8984375
- dt_raw: float32 [256, 4096], P('head', 'ctx'), may hold values from -2 to 4
- a_log: float32 [256], P('head'), may hold values from -12 to -3
- d_skip: float32 [256], P('head'), may hold values from 0.5 to 1.5
- conv_x: bfloat16 [4, 16384], P(None, 'head'), may hold values from -3 to 3
- conv_bc: bfloat16 [4, 2048], replicated, may hold values from -3 to 3
- norm_gain: float32 [16384], P('head'), may hold values from 0.5 to 1.5
- queries: bfloat16 [4096, 8192], P('ctx', 'head'), may hold values from -160 to 160
- keys_values: bfloat16 [2, 4096, 1024], P(None, 'ctx'), may hold values from -10 to 10
Outputs:
- ssm_out: bfloat16 [4096, 16384], P('ctx', 'head')
- attn_out: bfloat16 [4096, 8192], P('ctx', 'head')
The draws below stay inside these ranges and needn't reach their ends.
All inputs are finite; a program needn't handle non-finite values.
Results may differ from the reference program's by a relative error of at most 0.008.
Values may be sent and summed in bfloat16 or wider, within the bound.
A program may use at most 64 MiB of HBM per device.

```python
import math
import jax
import jax.numpy as jnp
from jax import lax

SSM_HEADS = 256
SSM_HEAD_DIM = 64
STATE = 128
GROUPS = 8
Q_HEADS = 64
KV_HEADS = 8
HEAD_DIM = 128
CONV = 4
BLOCK = 128
TOK_DEV = 256
TOKENS = 4096
N_CTX = 16


def draw_x_in(key, part):
    basic_key, row_key = jax.random.split(jax.random.fold_in(key, 11))
    per_group = SSM_HEADS // GROUPS
    columns = SSM_HEADS * SSM_HEAD_DIM
    head_of = jnp.arange(columns) // SSM_HEAD_DIM
    rising = jnp.power(3.0, (head_of % per_group).astype(jnp.float32) / max(per_group - 1, 1))
    row_scale = jnp.exp(jax.random.uniform(row_key, (TOKENS, 1), minval=0.0, maxval=math.log(10.0)))
    basic_draw = jnp.clip(jax.random.normal(basic_key, (TOKENS, columns)), -4.0, 4.0)
    return (0.5 * basic_draw * rising[None, :] * row_scale).astype(jnp.bfloat16)


def draw_dt_raw(key, part):
    token_key, device_key = jax.random.split(jax.random.fold_in(key, 13))
    device_count = TOKENS // TOK_DEV
    spread = math.log(2.0)
    per_device = jax.random.uniform(device_key, (SSM_HEADS, device_count), minval=-spread, maxval=spread)
    per_token = jax.random.uniform(token_key, (SSM_HEADS, TOKENS), minval=-spread, maxval=spread)
    target = jnp.exp(per_token + jnp.repeat(per_device, TOK_DEV, axis=1))
    return jnp.log(jnp.expm1(target))


def draw_a_log(key, part):
    pick_key, slow_key, fast_key = jax.random.split(jax.random.fold_in(key, 17), 3)
    chooser = jax.random.randint(pick_key, (SSM_HEADS,), 0, 10)
    slow_share = 5
    slow_rate = jax.random.uniform(slow_key, (SSM_HEADS,), minval=0.2, maxval=0.8) / TOKENS
    fast_rate = jax.random.uniform(fast_key, (SSM_HEADS,), minval=1.0 / 50.0, maxval=1.0 / 30.0)
    return jnp.log(jnp.where(chooser < slow_share, slow_rate, fast_rate))


def attention_pair(key):
    keys_key, value_key, query_key = jax.random.split(jax.random.fold_in(key, 23), 3)
    key_rows = 1.25 * jnp.clip(jax.random.normal(keys_key, (TOKENS, KV_HEADS, HEAD_DIM)), -6.0, 6.0)
    value_rows = jnp.clip(jax.random.normal(value_key, (TOKENS, KV_HEADS * HEAD_DIM)), -6.0, 6.0)
    query_rows = 2.0 * jnp.clip(jax.random.normal(query_key, (TOKENS, Q_HEADS, HEAD_DIM)), -6.0, 6.0)
    stacked = jnp.stack([key_rows.reshape(TOKENS, KV_HEADS * HEAD_DIM), value_rows])
    return (query_rows.reshape(TOKENS, Q_HEADS * HEAD_DIM), stacked)


def draw_queries(key, part):
    return attention_pair(key)[0].astype(jnp.bfloat16)


def draw_keys_values(key, part):
    return attention_pair(key)[1].astype(jnp.bfloat16)


def shard_levels(key, extent, cuts, smallest, largest):
    gain, own = 1.0, jax.random.fold_in(key, 6)
    for axis_at, blocks in cuts:
        draws = jnp.exp(jax.random.uniform(jax.random.fold_in(own, axis_at), (blocks,), jnp.float32, smallest / len(cuts), largest / len(cuts)))
        gain = gain * jnp.repeat(draws, extent[axis_at] // blocks).reshape([-1 if axis == axis_at else 1 for axis in range(len(extent))])
    return gain


def normal_values(key, dims, scale, most, cuts=(), kind=jnp.bfloat16):
    factor_of = shard_levels(key, dims, cuts, -0.22, 0.18) if cuts else 1.0
    values = jax.random.normal(key, dims, jnp.float32) * scale * factor_of
    return jnp.minimum(jnp.maximum(values, -most), most).astype(kind)


def setup_inputs(seed: int = 0) -> dict:
    seeds = jax.random.split(jax.random.key(seed), 12)
    return {
        "x_in": draw_x_in(jax.random.fold_in(seeds[11], 71), 0),
        "z_in": normal_values(seeds[1], (TOKENS, SSM_HEADS * SSM_HEAD_DIM), 1.0, 6.0, ((0, 16), (1, 32))),
        "bc_in": normal_values(seeds[2], (TOKENS, 2 * GROUPS * STATE), 0.15, 0.8984375, ((0, 16),)),
        "dt_raw": draw_dt_raw(jax.random.fold_in(seeds[11], 71), 0),
        "a_log": draw_a_log(jax.random.fold_in(seeds[11], 71), 0),
        "d_skip": jnp.clip(0.5 + 1.0 * jax.random.uniform(seeds[5], (SSM_HEADS,), jnp.float32) ** shard_levels(seeds[5], (SSM_HEADS,), ((0, 32),), -0.2, 0.2), 0.5, 1.5),
        "conv_x": normal_values(seeds[6], (CONV, SSM_HEADS * SSM_HEAD_DIM), CONV ** -0.5, 3.0, ((1, 32),)),
        "conv_bc": normal_values(seeds[7], (CONV, 2 * GROUPS * STATE), CONV ** -0.5, 3.0),
        "norm_gain": jnp.clip(1.0 + 0.1 * jax.random.normal(seeds[8], (SSM_HEADS * SSM_HEAD_DIM,), jnp.float32), 0.5, 1.5),
        "queries": draw_queries(jax.random.fold_in(seeds[11], 71), 0),
        "keys_values": draw_keys_values(jax.random.fold_in(seeds[11], 71), 0),
    }


EPSILON = 1e-05
NEGATIVE = -1e+30
HIGH = lax.Precision.HIGHEST

def widened(value):
    return lax.optimization_barrier(value).astype(jnp.float32)

def causal_conv(signal, conv_taps):
    rim_rows = conv_taps.shape[0] - 1
    padded = jnp.concatenate([jnp.zeros((rim_rows, signal.shape[1]), signal.dtype), signal], axis=0)
    total_sum = jnp.zeros(signal.shape, jnp.float32)
    for offset in range(conv_taps.shape[0]):
        total_sum = total_sum + padded[offset:offset + signal.shape[0]].astype(jnp.float32) * conv_taps[offset].astype(jnp.float32)
    return jax.nn.silu(total_sum).astype(jnp.bfloat16)

def reference(x_in, z_in, bc_in, dt_raw, a_log, d_skip, conv_x, conv_bc, norm_gain, queries, keys_values):
    per_group = SSM_HEADS // GROUPS
    block_count = TOKENS // BLOCK
    x_conv = causal_conv(x_in, conv_x)
    bc_conv = causal_conv(bc_in, conv_bc)
    step_size = jax.nn.softplus(dt_raw)
    log_rate = -jnp.exp(a_log)[:, None] * step_size
    x_blocks = widened(x_conv).reshape(block_count, BLOCK, SSM_HEADS, SSM_HEAD_DIM)
    wide_bc = widened(bc_conv)
    b_blocks = wide_bc[:, :GROUPS * STATE].reshape(block_count, BLOCK, GROUPS, STATE)
    c_blocks = wide_bc[:, GROUPS * STATE:].reshape(block_count, BLOCK, GROUPS, STATE)
    step_blocks = step_size.reshape(SSM_HEADS, block_count, BLOCK).transpose(1, 0, 2)
    rate_blocks = log_rate.reshape(SSM_HEADS, block_count, BLOCK).transpose(1, 0, 2)
    lower_mask = jnp.tril(jnp.ones((BLOCK, BLOCK), dtype=bool))

    def one_block(entering, operands):
        x_block, b_block, c_block, step_block, rate_block = operands
        cum_rate = jnp.cumsum(rate_block, axis=1)
        scores = jnp.einsum('tgn,sgn->gts', c_block, b_block, precision=HIGH)
        scores = jnp.repeat(scores, per_group, axis=0)
        rate_gap = jnp.minimum(cum_rate[:, :, None] - cum_rate[:, None, :], 0.0)
        decays = jnp.where(lower_mask, jnp.exp(rate_gap), 0.0)
        weights = (scores * decays * step_block[:, None, :]).astype(jnp.bfloat16)
        diag_term = jnp.einsum('hts,shp->thp', widened(weights), x_block, precision=HIGH)
        tail_decay = jnp.exp(cum_rate[:, -1:] - cum_rate) * step_block
        carried = (tail_decay.T[:, :, None] * x_block).astype(jnp.bfloat16)
        b_heads = jnp.repeat(b_block, per_group, axis=1)
        block_state = jnp.einsum('shp,shn->hpn', widened(carried), b_heads, precision=HIGH)
        c_heads = jnp.repeat(c_block, per_group, axis=1)
        reach_term = jnp.einsum('thn,hpn->thp', c_heads, entering, precision=HIGH)
        offdiag = reach_term * jnp.exp(cum_rate).T[:, :, None]
        leaving = jnp.exp(cum_rate[:, -1])[:, None, None] * entering + block_state
        return (leaving, diag_term + offdiag)
    initial = jnp.zeros((SSM_HEADS, SSM_HEAD_DIM, STATE), jnp.float32)
    _, mixed_out = lax.scan(one_block, initial, (x_blocks, b_blocks, c_blocks, step_blocks, rate_blocks))
    ssm_raw = mixed_out + d_skip[None, None, :, None] * x_blocks
    ssm_raw = ssm_raw.reshape(TOKENS, SSM_HEADS * SSM_HEAD_DIM)
    gated_out = ssm_raw * jax.nn.silu(z_in.astype(jnp.float32))
    grouped = gated_out.reshape(TOKENS, GROUPS, per_group * SSM_HEAD_DIM)
    mean_square = lax.optimization_barrier(jnp.mean(grouped * grouped, axis=2))
    normed = grouped * lax.rsqrt(mean_square + EPSILON)[:, :, None]
    ssm_out = (normed.reshape(TOKENS, SSM_HEADS * SSM_HEAD_DIM) * norm_gain[None, :]).astype(jnp.bfloat16)
    per_kv = Q_HEADS // KV_HEADS
    score_scale = 1.0 / math.sqrt(HEAD_DIM)
    key_heads = keys_values[0].reshape(TOKENS, KV_HEADS, HEAD_DIM)
    value_heads = keys_values[1].reshape(TOKENS, KV_HEADS, HEAD_DIM)
    grouped_q = queries.reshape(TOKENS, KV_HEADS, per_kv, HEAD_DIM)
    pieces = []
    for block_index in range(N_CTX):
        low_row = block_index * TOK_DEV
        high_row = low_row + TOK_DEV
        visible = jnp.arange(low_row, high_row)[:, None] >= jnp.arange(high_row)[None, :]

        def per_head(operands):
            q_part, k_part, v_part = operands
            logits = jnp.einsum('tjd,sd->jts', widened(q_part), widened(k_part), precision=HIGH) * score_scale
            logits = jnp.where(visible[None], logits, NEGATIVE)
            row_top = lax.optimization_barrier(jnp.max(logits, axis=2, keepdims=True))
            exp_scores = jnp.where(visible[None], jnp.exp(logits - row_top), 0.0)
            row_total = lax.optimization_barrier(jnp.sum(exp_scores, axis=2))
            weighted = jnp.einsum('jts,sd->tjd', widened(exp_scores.astype(jnp.bfloat16)), widened(v_part), precision=HIGH)
            return weighted / row_total.T[:, :, None]
        result = lax.map(per_head, (grouped_q[low_row:high_row].transpose(1, 0, 2, 3), key_heads[:high_row].transpose(1, 0, 2), value_heads[:high_row].transpose(1, 0, 2)))
        pieces.append(result.transpose(1, 0, 2, 3).reshape(TOK_DEV, Q_HEADS * HEAD_DIM))
    attn_out = jnp.concatenate(pieces, axis=0).astype(jnp.bfloat16)
    return (ssm_out, attn_out)
```

```python
import functools
import math

import jax
import jax.numpy as jnp
from jax import lax
from jax.experimental import pallas as pl
from jax.experimental.pallas import tpu as pltpu
from jax.sharding import PartitionSpec as P

GROUPS = 8
STATE = 128
HEAD_DIM = 128
CONV = 4
TOK = 256
HEADS = 8
CHAN = 512
N_CTX = 16
ROWS_Z = 8
HALF = CHAN // 2
SLICE = 16
QUART = TOK // 4
EPSILON = 1e-05
NEGATIVE = -1e30
HIGH = lax.Precision.HIGHEST
MESH = pl.DeviceIdType.MESH
F32 = jnp.float32
BF16 = jnp.bfloat16
PEERS = ((0, 1), (1, 0), (1, 1))
EXP_SCALE = math.log2(math.e) / math.sqrt(HEAD_DIM)


def silu(v):
    return v / (1.0 + jnp.exp(-v))


def conv_rows(pad_ref, taps, cols):
    total = jnp.zeros((TOK, cols.size), F32)
    for k in range(CONV):
        total = total + pad_ref[5 + k : 5 + k + TOK, cols] * taps[k : k + 1]
    return silu(total)


def kernel(
    x_hbm, z_hbm, bc_hbm, dt_ref, alog_ref, dskip_ref, cx_ref, cbc_ref, gain_ref, q_hbm, kv_hbm,
    ssm_ref, attn_ref,
    x_v, z_v, b_v, c_v, q_v, q2_v, kvbuf, halo_x, halo_bc, pad_x, pad_bc,
    st_send, in_a, out_b, in_b, dec_send, dec_in, pre_v, sz_v, ecx_v, cb_v, sq_v,
    m_v, l_v, o_v,
    loc, h_s, h_r, d_s, d_r, a_s, a_r, b_s, b_r, q_s, q_r, s1_s, s1_r, x_s, x_r, c_s, c_r,
):
    c = lax.axis_index("ctx")
    hd = lax.axis_index("head")
    z, xh = lax.div(c, 2), lax.rem(c, 2)
    y, qi = lax.div(hd, 4), lax.rem(hd, 4)
    xl, core = lax.div(qi, 2), lax.rem(qi, 2)
    flip_c = 1 - 2 * xh
    flip_l = 2 * (1 - 2 * xl)
    sib = hd + 1 - 2 * core
    ycol = pl.multiple_of(y * 128, 128)
    ycol2 = pl.multiple_of(GROUPS * STATE + y * 128, 128)

    def remote(src, dst, ss, rs, ctx, head):
        return pltpu.make_async_remote_copy(
            src_ref=src, dst_ref=dst, send_sem=ss, recv_sem=rs,
            device_id=(ctx, head), device_id_type=MESH,
        )

    loads = [
        pltpu.make_async_copy(x_hbm, x_v, loc.at[0]),
        pltpu.make_async_copy(bc_hbm.at[:, pl.ds(ycol, 128)], b_v, loc.at[1]),
        pltpu.make_async_copy(bc_hbm.at[:, pl.ds(ycol2, 128)], c_v, loc.at[2]),
        pltpu.make_async_copy(q_hbm, q_v, loc.at[3]),
        pltpu.make_async_copy(z_hbm, z_v, loc.at[4]),
    ]
    for i in range(4):
        loads.append(
            pltpu.make_async_copy(
                kv_hbm.at[:, pl.ds(QUART * i, QUART), pl.ds(ycol, 128)],
                kvbuf.at[:, z, xh, i // 2, i % 2],
                loc.at[5 + i],
            )
        )
    for cp in loads:
        cp.start()

    barrier = pltpu.get_barrier_semaphore()

    def greet(ctx, head):
        pl.semaphore_signal(barrier, inc=1, device_id=(ctx, head), device_id_type=MESH)

    def greet_ctx(d, carry):
        greet(lax.rem(c + d, N_CTX), hd)
        return carry

    lax.fori_loop(1, N_CTX, greet_ctx, 0)
    greet(c, hd + flip_l)
    greet(c + flip_c, hd + flip_l)
    greet(c, sib)
    greet(c, sib + flip_l)

    a_log = jnp.zeros((HEADS, 1), F32)
    head_row = lax.broadcasted_iota(jnp.int32, (HEADS, 1), 0)
    for h in range(HEADS):
        a_log = jnp.where(head_row == h, alog_ref[h], a_log)
    step = jnp.log(1.0 + jnp.exp(dt_ref[...]))
    cum = -jnp.exp(a_log) * step
    lane = lax.broadcasted_iota(jnp.int32, (HEADS, TOK), 1)
    shift = 1
    while shift < TOK:
        cum = cum + jnp.where(lane >= shift, pltpu.roll(cum, shift, 1), 0.0)
        shift *= 2
    last = cum[:, TOK - 1 : TOK]
    of_head = (
        lax.div(lax.broadcasted_iota(jnp.int32, (HEADS, CHAN), 1), CHAN // HEADS)
        == lax.broadcasted_iota(jnp.int32, (HEADS, CHAN), 0)
    )
    spread = jnp.where(of_head, 1.0, 0.0).astype(F32)
    total_row = jnp.sum(jnp.where(of_head, last, 0.0), axis=0, keepdims=True)
    for half in range(2):
        dec_send[half] = total_row[:, half * HALF : (half + 1) * HALF]
    own_half = lax.div(c, 8)

    pl.semaphore_wait(barrier, N_CTX - 1 + 4)

    def halo_copies():
        nxt = lax.rem(c + 1, N_CTX)
        tail = pl.ds(TOK - 16, 16)
        return [
            remote(x_hbm.at[tail, :], halo_x, h_s.at[0], h_r.at[0], nxt, hd),
            remote(bc_hbm.at[tail, pl.ds(ycol, 128)], halo_bc.at[0], h_s.at[1], h_r.at[1], nxt, hd),
            remote(bc_hbm.at[tail, pl.ds(ycol2, 128)], halo_bc.at[1], h_s.at[2], h_r.at[2], nxt, hd),
        ]

    @pl.when(c < N_CTX - 1)
    def _():
        for cp in halo_copies():
            cp.start()

    def dec_copy(d):
        to = lax.rem(c + d, N_CTX)
        return remote(dec_send.at[lax.div(to, 8)], dec_in.at[c], d_s.at[d], d_r.at[d], to, hd)

    def dec_start(d, carry):
        dec_copy(d).start()
        return carry

    lax.fori_loop(1, N_CTX, dec_start, 0)
    dec_in[c] = dec_send[own_half]

    def kv1_copy(d):
        return remote(
            kv_hbm.at[:, pl.ds(pl.multiple_of(QUART * qi, QUART), QUART), pl.ds(ycol, 128)],
            kvbuf.at[:, z, xh, xl, core],
            s1_s.at[d], s1_r.at[d], lax.rem(c + 2 * d, N_CTX), hd,
        )

    def kv1_start(d, carry):
        kv1_copy(d).start()
        return carry

    lax.fori_loop(1, ROWS_Z - z, kv1_start, 0)

    def x_copy(d, p):
        fh, fl = PEERS[p]
        piece = kvbuf.at[:, z - d, xh, xl, core]
        return remote(piece, piece, x_s.at[d, p], x_r.at[d, p], c + fh * flip_c, hd + fl * flip_l)

    def core_copy(d):
        piece = kvbuf.at[:, z - d, :, :, core]
        return remote(piece, piece, c_s.at[d], c_r.at[d], c, sib)

    def core_copy_own():
        piece = kvbuf.at[:, z, 1 - xh, :, core]
        return remote(piece, piece, c_s.at[0], c_r.at[0], c, sib)

    for i in range(4):
        loads[5 + i].wait()
    for p in (1, 2):
        x_copy(0, p).start()

    loads[3].wait()
    q2_v[0:TOK] = q_v[:, :HEAD_DIM]
    q2_v[TOK:] = q_v[:, HEAD_DIM:]

    def attend(keys, values, mask, first):
        logits = lax.dot_general(
            keys, q2_v[...], (((1,), (1,)), ((), ())), preferred_element_type=F32
        )
        if mask is not None:
            logits = jnp.where(mask, logits, NEGATIVE)
        top = jnp.max(logits, axis=0, keepdims=True)
        if not first:
            top = jnp.maximum(m_v[...], top)
        grown = jnp.exp2((logits - top) * EXP_SCALE)
        if mask is not None:
            grown = jnp.where(mask, grown, 0.0)
        den = jnp.sum(grown, axis=0, keepdims=True)
        got = jnp.dot(values.T, grown.astype(BF16), preferred_element_type=F32)
        if first:
            l_v[...] = den
            o_v[...] = got
        else:
            shrink = jnp.exp2((m_v[...] - top) * EXP_SCALE)
            l_v[...] = l_v[...] * shrink + den
            o_v[...] = o_v[...] * shrink + got
        m_v[...] = top

    key_at = lax.broadcasted_iota(jnp.int32, (TOK, 2 * TOK), 0)
    query_at = lax.rem(lax.broadcasted_iota(jnp.int32, (TOK, 2 * TOK), 1), TOK)
    attend(
        kvbuf[0, z, xh].reshape(TOK, HEAD_DIM), kvbuf[1, z, xh].reshape(TOK, HEAD_DIM),
        key_at <= query_at, True,
    )

    loads[0].wait()
    loads[1].wait()
    loads[2].wait()

    @pl.when(c > 0)
    def _():
        for cp in halo_copies():
            cp.wait_recv()

    @pl.when(c == 0)
    def _():
        halo_x[...] = jnp.zeros_like(halo_x)
        halo_bc[...] = jnp.zeros_like(halo_bc)

    pad_bc[8:, 0:STATE] = b_v[...].astype(F32)
    pad_bc[8:, STATE:] = c_v[...].astype(F32)
    pad_bc[0:8, 0:STATE] = halo_bc[0].astype(F32)[8:16]
    pad_bc[0:8, STATE:] = halo_bc[1].astype(F32)[8:16]
    pad_x[8:] = x_v[...].astype(F32)
    pad_x[0:8] = halo_x[...].astype(F32)[8:16]
    b_conv = conv_rows(pad_bc, cbc_ref[:, pl.ds(ycol, 128)].astype(F32), pl.ds(0, STATE))
    b_t = b_conv.T.astype(BF16)
    c_conv = conv_rows(pad_bc, cbc_ref[:, pl.ds(ycol2, 128)].astype(F32), pl.ds(STATE, STATE))
    cb_v[...] = c_conv.astype(BF16)
    x_conv = conv_rows(pad_x, cx_ref[...].astype(F32), pl.ds(0, CHAN)).astype(BF16)
    x_v[...] = x_conv
    wide_x = x_conv.astype(F32)

    tail = jnp.exp(last - cum) * step
    tail_x = jnp.dot(tail.T, spread, precision=HIGH, preferred_element_type=F32)
    carried = (tail_x * wide_x).astype(BF16)
    state = jnp.dot(b_t, carried, preferred_element_type=F32).astype(BF16)
    for half in range(2):
        st_send[8 * half : 8 * half + 8] = state[:, half * HALF : (half + 1) * HALF].reshape(
            8, SLICE, HALF
        )

    def a_copy(d):
        to = lax.rem(c + d, N_CTX)
        return remote(st_send.at[to], in_a.at[c], a_s.at[d], a_r.at[d], to, hd)

    def a_start(d, carry):
        a_copy(d).start()
        return carry

    lax.fori_loop(1, N_CTX, a_start, 0)
    in_a[c] = st_send[c]

    def forward(d, carry):
        kv1_copy(d).wait_recv()
        for p in range(3):
            x_copy(d, p).start()
        return carry

    lax.fori_loop(1, z + 1, forward, 0)

    scores = jnp.dot(cb_v[...], b_t, preferred_element_type=F32)
    t_at = lax.broadcasted_iota(jnp.int32, (TOK, TOK), 0)
    s_at = lax.broadcasted_iota(jnp.int32, (TOK, TOK), 1)
    scores = jnp.where(s_at <= t_at, scores, 0.0)
    cum_t = cum.T
    skip_row = jnp.zeros((1, CHAN), F32)
    head_of_lane = lax.div(lax.broadcasted_iota(jnp.int32, (1, CHAN), 1), CHAN // HEADS)
    for h in range(HEADS):
        skip_row = jnp.where(head_of_lane == h, dskip_ref[h], skip_row)
    left = lax.broadcasted_iota(jnp.int32, (TOK, 128), 1) < 64
    for pair in range(HEADS // 2):
        cols = slice(128 * pair, 128 * pair + 128)
        both = []
        for h in (2 * pair, 2 * pair + 1):
            gap = jnp.minimum(cum_t[:, h : h + 1] - cum[h : h + 1, :], 0.0)
            weights = (scores * jnp.exp(gap) * step[h : h + 1, :]).astype(BF16)
            both.append(jnp.dot(weights, x_v[:, cols], preferred_element_type=F32))
        pre_v[:, cols] = (
            jnp.where(left, both[0], both[1])
            + skip_row[:, cols] * x_v[:, cols].astype(F32)
        )
    ecx_v[...] = jnp.dot(jnp.exp(cum).T, spread, precision=HIGH, preferred_element_type=F32)
    loads[4].wait()
    sz_v[...] = silu(z_v[...].astype(F32))

    def a_wait(d, carry):
        dec_copy(d).wait_recv()
        a_copy(d).wait_recv()
        return carry

    lax.fori_loop(1, N_CTX, a_wait, 0)
    running = jnp.zeros((SLICE, HALF), F32)
    for k in range(N_CTX):
        out_b[k] = running.astype(BF16)
        running = jnp.exp(dec_in[k]) * running + in_a[k].astype(F32)

    def b_copy(d):
        to = lax.rem(c + d, N_CTX)
        return remote(out_b.at[to], in_b.at[c], b_s.at[d], b_r.at[d], to, hd)

    def b_start(d, carry):
        b_copy(d).start()
        return carry

    lax.fori_loop(1, N_CTX, b_start, 0)
    in_b[c] = out_b[c]

    for p in (1, 2):
        x_copy(0, p).wait_recv()
    core_copy_own().start()

    def to_core(d, carry):
        for p in range(3):
            x_copy(d, p).wait_recv()
        core_copy(d).start()
        return carry

    lax.fori_loop(1, z + 1, to_core, 0)

    def b_wait(d, carry):
        b_copy(d).wait_recv()
        return carry

    lax.fori_loop(1, N_CTX, b_wait, 0)
    squares = jnp.zeros((TOK, 128), F32)
    for half in range(2):
        cols = slice(half * HALF, (half + 1) * HALF)
        entering = in_b[8 * half : 8 * half + 8].reshape(STATE, HALF)
        reach = jnp.dot(cb_v[...], entering, preferred_element_type=F32)
        gated = (pre_v[:, cols] + ecx_v[:, cols] * reach) * sz_v[:, cols]
        pre_v[:, cols] = gated
        squares = squares + gated[:, :128] * gated[:, :128] + gated[:, 128:] * gated[:, 128:]
    sq_v[0] = jnp.sum(squares.T, axis=0, keepdims=True)

    def quad_copies():
        return [
            remote(sq_v.at[0], sq_v.at[1], q_s.at[0], q_r.at[0], c, sib),
            remote(sq_v.at[0], sq_v.at[2], q_s.at[1], q_r.at[1], c, hd + flip_l),
            remote(sq_v.at[0], sq_v.at[3], q_s.at[2], q_r.at[2], c, sib + flip_l),
        ]

    for cp in quad_copies():
        cp.start()

    core_copy_own().wait_recv()

    @pl.when(xh == 1)
    def _():
        attend(
            kvbuf[0, z, 0].reshape(TOK, HEAD_DIM), kvbuf[1, z, 0].reshape(TOK, HEAD_DIM),
            None, False,
        )

    def attend_row(d, carry):
        core_copy(d).wait_recv()
        attend(
            kvbuf[0, z - d].reshape(2 * TOK, HEAD_DIM), kvbuf[1, z - d].reshape(2 * TOK, HEAD_DIM),
            None, False,
        )
        return carry

    lax.fori_loop(1, z + 1, attend_row, 0)
    result = o_v[...] / l_v[...]
    for h in range(2):
        attn_ref[:, h * HEAD_DIM : (h + 1) * HEAD_DIM] = result[
            :, h * TOK : (h + 1) * TOK
        ].T.astype(BF16)

    for cp in quad_copies():
        cp.wait_recv()
    group_total = sq_v[0] + sq_v[1] + sq_v[2] + sq_v[3]
    scale = lax.rsqrt(group_total * (1.0 / 2048.0) + EPSILON)
    scale_col = jnp.broadcast_to(scale, (8, TOK)).T[:, 0:1]
    ssm_ref[...] = (pre_v[...] * scale_col * gain_ref[...]).astype(BF16)

    @pl.when(c < N_CTX - 1)
    def _():
        for cp in halo_copies():
            cp.wait_send()

    def sent(d, carry):
        dec_copy(d).wait_send()
        a_copy(d).wait_send()
        b_copy(d).wait_send()
        return carry

    lax.fori_loop(1, N_CTX, sent, 0)

    def kv1_sent(d, carry):
        kv1_copy(d).wait_send()
        return carry

    lax.fori_loop(1, ROWS_Z - z, kv1_sent, 0)

    def row_sent(d, carry):
        for p in range(3):
            x_copy(d, p).wait_send()
        core_copy(d).wait_send()
        return carry

    lax.fori_loop(1, z + 1, row_sent, 0)
    for p in (1, 2):
        x_copy(0, p).wait_send()
    core_copy_own().wait_send()
    for cp in quad_copies():
        cp.wait_send()


def local(
    x_in, z_in, bc_in, dt_raw, a_log, d_skip, conv_x, conv_bc, norm_gain, queries, keys_values
):
    any_spec = pl.BlockSpec(memory_space=pl.ANY)
    vmem = pl.BlockSpec(memory_space=pltpu.VMEM)
    smem = pl.BlockSpec(memory_space=pltpu.SMEM)
    dma = pltpu.SemaphoreType.DMA
    return pl.pallas_call(
        kernel,
        out_shape=(
            jax.ShapeDtypeStruct((TOK, CHAN), BF16),
            jax.ShapeDtypeStruct((TOK, 2 * HEAD_DIM), BF16),
        ),
        in_specs=[
            any_spec, any_spec, any_spec, vmem, smem, smem, vmem, vmem, vmem, any_spec, any_spec,
        ],
        out_specs=(vmem, vmem),
        scratch_shapes=[
            pltpu.VMEM((TOK, CHAN), BF16),
            pltpu.VMEM((TOK, CHAN), BF16),
            pltpu.VMEM((TOK, STATE), BF16),
            pltpu.VMEM((TOK, STATE), BF16),
            pltpu.VMEM((TOK, 2 * HEAD_DIM), BF16),
            pltpu.VMEM((2 * TOK, HEAD_DIM), BF16),
            pltpu.VMEM((2, ROWS_Z, 2, 2, 2, QUART, HEAD_DIM), BF16),
            pltpu.VMEM((16, CHAN), BF16),
            pltpu.VMEM((2, 16, STATE), BF16),
            pltpu.VMEM((8 + TOK, CHAN), F32),
            pltpu.VMEM((8 + TOK, 2 * STATE), F32),
            pltpu.VMEM((N_CTX, SLICE, HALF), BF16),
            pltpu.VMEM((N_CTX, SLICE, HALF), BF16),
            pltpu.VMEM((N_CTX, SLICE, HALF), BF16),
            pltpu.VMEM((N_CTX, SLICE, HALF), BF16),
            pltpu.VMEM((2, 1, HALF), F32),
            pltpu.VMEM((N_CTX, 1, HALF), F32),
            pltpu.VMEM((TOK, CHAN), F32),
            pltpu.VMEM((TOK, CHAN), F32),
            pltpu.VMEM((TOK, CHAN), F32),
            pltpu.VMEM((TOK, STATE), BF16),
            pltpu.VMEM((4, 1, TOK), F32),
            pltpu.VMEM((1, 2 * TOK), F32),
            pltpu.VMEM((1, 2 * TOK), F32),
            pltpu.VMEM((HEAD_DIM, 2 * TOK), F32),
            dma((9,)), dma((3,)), dma((3,)),
            dma((N_CTX,)), dma((N_CTX,)), dma((N_CTX,)), dma((N_CTX,)),
            dma((N_CTX,)), dma((N_CTX,)),
            dma((3,)), dma((3,)), dma((ROWS_Z,)), dma((ROWS_Z,)),
            dma((ROWS_Z, 3)), dma((ROWS_Z, 3)), dma((ROWS_Z,)), dma((ROWS_Z,)),
        ],
        compiler_params=pltpu.CompilerParams(
            collective_id=0, has_side_effects=True, vmem_limit_bytes=40 * 1024 * 1024
        ),
        name="mixer",
    )(
        x_in, z_in, bc_in, dt_raw, a_log, d_skip, conv_x, conv_bc,
        norm_gain.reshape(1, CHAN), queries, keys_values,
    )


def solution(mesh):
    placed = (
        P("ctx", "head"),
        P("ctx", "head"),
        P("ctx", None),
        P("head", "ctx"),
        P("head"),
        P("head"),
        P(None, "head"),
        P(),
        P("head"),
        P("ctx", "head"),
        P(None, "ctx", None),
    )
    return jax.shard_map(
        local,
        mesh=mesh,
        in_specs=placed,
        out_specs=(P("ctx", "head"), P("ctx", "head")),
        check_vma=False,
    )
```

```python
import functools
import math

import jax
import jax.numpy as jnp
from jax import lax
from jax.experimental import pallas as pl
from jax.experimental.pallas import tpu as pltpu
from jax.sharding import PartitionSpec as P

GROUPS = 8
STATE = 128
HEAD_DIM = 128
CONV = 4
TOK = 256
HEADS = 8
CHAN = 512
N_CTX = 16
BLOCK = 128
ROWS_Z = 8
SLICE = STATE // 4
QUART = TOK // 4
EPSILON = 1e-05
NEGATIVE = -1e30
HIGH = lax.Precision.HIGHEST
MESH = pl.DeviceIdType.MESH
F32 = jnp.float32
BF16 = jnp.bfloat16
PEERS = ((0, 1), (1, 0), (1, 1))
EXP_SCALE = math.log2(math.e) / math.sqrt(HEAD_DIM)


def silu(v):
    return v / (1.0 + jnp.exp(-v))


def conv_rows(pad_ref, taps, cols, rows):
    total = jnp.zeros((rows, cols.size), F32)
    for k in range(CONV):
        total = total + pad_ref[5 + k : 5 + k + rows, cols] * taps[k : k + 1]
    return silu(total)


def kernel(
    x_hbm, z_hbm, bc_hbm, dt_hbm, alog_hbm, dskip_hbm, cx_hbm, cbc_hbm, gain_hbm, q_hbm, kv_hbm,
    ssm_hbm, attn_hbm,
    dt_ref, alog_ref, dskip_ref, cx_ref, cbc_ref, gain_ref,
    x_v, z_v, b_v, c_v, q_v, q2_v, kvbuf, halo_x, halo_bc, pad_x, pad_bc, bf_v,
    st_send, in_a, out_b, in_b, e_out, e_in, dec_send, dec_in, pre_v, sz_v, ecx_v, cb_v, sq_v,
    m_v, l_v, o_v, ssm_v, attn_v,
    loc, h_s, h_r, d_s, d_r, a_s, a_r, b_s, b_r, e_s, e_r, q_s, q_r, s1_s, s1_r,
    x_s, x_r, c_s, c_r, rdy,
):
    c = lax.axis_index("ctx")
    hd = lax.axis_index("head")
    z, xh = lax.div(c, 2), lax.rem(c, 2)
    grp, mem = lax.div(c, 4), lax.rem(c, 4)
    zodd = lax.rem(z, 2)
    y, qi = lax.div(hd, 4), lax.rem(hd, 4)
    xl, core = lax.div(qi, 2), lax.rem(qi, 2)
    flip_c = 1 - 2 * xh
    flip_l = 2 * (1 - 2 * xl)
    sib = hd + 1 - 2 * core
    ycol = pl.multiple_of(y * 128, 128)
    ycol2 = pl.multiple_of(GROUPS * STATE + y * 128, 128)
    mates = [lax.rem(mem + e, 4) for e in (1, 2, 3)]

    def remote(src, dst, ss, rs, ctx, head):
        return pltpu.make_async_remote_copy(
            src_ref=src, dst_ref=dst, send_sem=ss, recv_sem=rs,
            device_id=(ctx, head), device_id_type=MESH,
        )

    small = [
        pltpu.make_async_copy(src, dst, loc.at[i])
        for i, (src, dst) in enumerate(
            (
                (dt_hbm, dt_ref), (alog_hbm, alog_ref), (dskip_hbm, dskip_ref),
                (cx_hbm, cx_ref), (cbc_hbm, cbc_ref), (gain_hbm, gain_ref),
            )
        )
    ]
    load_x = pltpu.make_async_copy(x_hbm, x_v, loc.at[6])
    load_b = pltpu.make_async_copy(bc_hbm.at[:, pl.ds(ycol, 128)], b_v, loc.at[7])
    load_c = pltpu.make_async_copy(bc_hbm.at[:, pl.ds(ycol2, 128)], c_v, loc.at[8])
    load_q = pltpu.make_async_copy(q_hbm, q_v, loc.at[9])
    load_z = pltpu.make_async_copy(z_hbm, z_v, loc.at[10])
    load_kv = pltpu.make_async_copy(
        kv_hbm.at[:, :, :, :, pl.ds(ycol, 128)], kvbuf.at[:, z, xh], loc.at[11]
    )
    for cp in small + [load_b, load_c, load_x, load_kv, load_q, load_z]:
        cp.start()

    barrier = pltpu.get_barrier_semaphore()

    def greet(ctx, head):
        pl.semaphore_signal(barrier, inc=1, device_id=(ctx, head), device_id_type=MESH)

    for to in mates:
        greet(c - mem + to, hd)
    greet(c, sib)
    greet(c, hd + flip_l)
    greet(c, sib + flip_l)
    greet(c + flip_c, hd + flip_l)

    @pl.when((mem == 0) & (c > 0))
    def _():
        greet(c - 1, hd)

    def greet_later(d, carry):
        greet(c + 2 * d, hd)
        return carry

    lax.fori_loop(2 - zodd, ROWS_Z - z, greet_later, 0)

    for cp in small:
        cp.wait()
    a_log = jnp.zeros((HEADS, 1), F32)
    head_row = lax.broadcasted_iota(jnp.int32, (HEADS, 1), 0)
    for h in range(HEADS):
        a_log = jnp.where(head_row == h, alog_ref[h], a_log)
    step = jnp.log(1.0 + jnp.exp(dt_ref[...]))
    cum = -jnp.exp(a_log) * step
    lane = lax.broadcasted_iota(jnp.int32, (HEADS, TOK), 1)
    shift = 1
    while shift < TOK:
        cum = cum + jnp.where(lane >= shift, pltpu.roll(cum, shift, 1), 0.0)
        shift *= 2
    last = cum[:, TOK - 1 : TOK]
    of_head = (
        lax.div(lax.broadcasted_iota(jnp.int32, (HEADS, CHAN), 1), CHAN // HEADS)
        == lax.broadcasted_iota(jnp.int32, (HEADS, CHAN), 0)
    )
    spread = jnp.where(of_head, 1.0, 0.0).astype(F32)
    dec_send[...] = jnp.sum(jnp.where(of_head, last, 0.0), axis=0, keepdims=True)
    dec_in[mem] = dec_send[...]
    tail = jnp.exp(last - cum) * step
    tail_x = jnp.dot(tail.T, spread, precision=HIGH, preferred_element_type=F32)

    taps_b = cbc_ref[:, pl.ds(ycol, 128)].astype(F32)
    taps_c = cbc_ref[:, pl.ds(ycol2, 128)].astype(F32)
    taps_x = cx_ref[...].astype(F32)
    pad_bc[0:8] = jnp.zeros((8, 2 * STATE), F32)
    pad_x[0:8] = jnp.zeros((8, CHAN), F32)
    load_b.wait()
    load_c.wait()
    pad_bc[8:, 0:STATE] = b_v[...].astype(F32)
    pad_bc[8:, STATE:] = c_v[...].astype(F32)

    def convolve(rows):
        bf_v[0:rows] = conv_rows(pad_bc, taps_b, pl.ds(0, STATE), rows)
        cb_v[0:rows] = conv_rows(pad_bc, taps_c, pl.ds(STATE, STATE), rows).astype(BF16)
        x_v[0:rows] = conv_rows(pad_x, taps_x, pl.ds(0, CHAN), rows).astype(BF16)

    load_x.wait()
    pad_x[8:] = x_v[...].astype(F32)
    convolve(TOK)

    greeted = 3 + 4 + 2 * grp + jnp.where((mem == 3) & (c < N_CTX - 1), 1, 0)
    pl.semaphore_wait(barrier, greeted)

    def halo_copies():
        tail_rows = pl.ds(TOK - 16, 16)
        return [
            remote(x_hbm.at[tail_rows, :], halo_x, h_s.at[0], h_r.at[0], c + 1, hd),
            remote(
                bc_hbm.at[tail_rows, pl.ds(ycol, 128)], halo_bc.at[0],
                h_s.at[1], h_r.at[1], c + 1, hd,
            ),
            remote(
                bc_hbm.at[tail_rows, pl.ds(ycol2, 128)], halo_bc.at[1],
                h_s.at[2], h_r.at[2], c + 1, hd,
            ),
        ]

    @pl.when(c < N_CTX - 1)
    def _():
        for cp in halo_copies():
            cp.start()

    def dec_copy(to):
        return remote(dec_send, dec_in.at[mem], d_s, d_r, c - mem + to, hd)

    for to in mates:
        dec_copy(to).start()

    for far in (1, 2, 3):

        @pl.when(grp >= far)
        def _():
            for odd in range(2):
                pl.semaphore_signal(
                    rdy.at[far - 1], inc=1, device_id=(4 * (grp - far) + 2 * odd + xh, hd),
                    device_id_type=MESH,
                )

    def kv1_copy(d):
        return remote(
            kvbuf.at[:, z, xh, xl, core], kvbuf.at[:, z, xh, xl, core],
            s1_s.at[d], s1_r.at[d], c + 2 * d, hd,
        )

    def kv1_got(d):
        piece = kvbuf.at[:, z - d, xh, xl, core]
        return remote(piece, piece, s1_s.at[d], s1_r.at[d], c, sib)

    def kv1_group(far):
        @pl.when(grp + far < 4)
        def _():
            pl.semaphore_wait(rdy.at[far - 1], 2)
            for odd in range(2):
                kv1_copy(2 * far + odd - zodd).start()

    def x_copy(d, p):
        fh, fl = PEERS[p]
        piece = kvbuf.at[:, z - d, xh, xl, core]
        return remote(piece, piece, x_s.at[d, p], x_r.at[d, p], c + fh * flip_c, hd + fl * flip_l)

    def core_copy(d):
        piece = kvbuf.at[:, z - d, :, :, core]
        return remote(piece, piece, c_s.at[d], c_r.at[d], c, sib)

    def core_copy_own():
        piece = kvbuf.at[:, z, 1 - xh, :, core]
        return remote(piece, piece, c_s.at[0], c_r.at[0], c, sib)

    @pl.when(c > 0)
    def _():
        for cp in halo_copies():
            cp.wait_recv()
        pad_bc[0:8, 0:STATE] = halo_bc[0].astype(F32)[8:16]
        pad_bc[0:8, STATE:] = halo_bc[1].astype(F32)[8:16]
        pad_x[0:8] = halo_x[...].astype(F32)[8:16]
        convolve(16)

    b_t = bf_v[...].T.astype(BF16)
    carried = (tail_x * x_v[...].astype(F32)).astype(BF16)
    state = jnp.dot(b_t, carried, preferred_element_type=F32).astype(BF16)
    st_send[...] = state.reshape(4, SLICE, CHAN)

    def a_copy(to):
        return remote(st_send.at[to], in_a.at[mem], a_s, a_r, c - mem + to, hd)

    for to in mates:
        a_copy(to).start()
    in_a[mem] = st_send[mem]

    load_kv.wait()
    for p in (1, 2):
        x_copy(0, p).start()

    @pl.when(zodd == 0)
    def _():
        kv1_copy(1).start()

    kv1_group(1)

    scores = jnp.dot(cb_v[...], b_t, preferred_element_type=F32)
    t_at = lax.broadcasted_iota(jnp.int32, (TOK, TOK), 0)
    s_at = lax.broadcasted_iota(jnp.int32, (TOK, TOK), 1)
    scores = jnp.where(s_at <= t_at, scores, 0.0)
    cum_t = cum.T
    skip_row = jnp.zeros((1, CHAN), F32)
    head_of_lane = lax.div(lax.broadcasted_iota(jnp.int32, (1, CHAN), 1), CHAN // HEADS)
    for h in range(HEADS):
        skip_row = jnp.where(head_of_lane == h, dskip_ref[h], skip_row)
    left = lax.broadcasted_iota(jnp.int32, (BLOCK, 128), 1) < 64
    for low in (0, BLOCK):
        rows, upto = slice(low, low + BLOCK), low + BLOCK
        for pair in range(HEADS // 2):
            cols = slice(128 * pair, 128 * pair + 128)
            both = []
            for h in (2 * pair, 2 * pair + 1):
                gap = jnp.minimum(cum_t[rows, h : h + 1] - cum[h : h + 1, :upto], 0.0)
                weights = (scores[rows, :upto] * jnp.exp(gap) * step[h : h + 1, :upto]).astype(BF16)
                both.append(jnp.dot(weights, x_v[:upto, cols], preferred_element_type=F32))
            pre_v[rows, cols] = (
                jnp.where(left, both[0], both[1])
                + skip_row[:, cols] * x_v[rows, cols].astype(F32)
            )
    ecx_v[...] = jnp.dot(jnp.exp(cum).T, spread, precision=HIGH, preferred_element_type=F32)
    load_z.wait()
    sz_v[...] = silu(z_v[...].astype(F32))

    three = pl.ds(0, 3)

    def e_copy():
        return remote(e_out, e_in, e_s, e_r, c + 4, hd)

    remote(dec_in.at[three], dec_in.at[three], d_s, d_r, c, sib).wait_recv()
    remote(st_send.at[three], in_a.at[three], a_s, a_r, c, sib).wait_recv()

    @pl.when(grp > 0)
    def _():
        e_copy().wait_recv()

    @pl.when(grp == 0)
    def _():
        e_in[...] = jnp.zeros_like(e_in)

    running = e_in[...].astype(F32)
    for k in range(4):
        out_b[k] = running.astype(BF16)
        running = jnp.exp(dec_in[k]) * running + in_a[k].astype(F32)
    e_out[...] = running.astype(BF16)

    @pl.when(grp < 3)
    def _():
        e_copy().start()

    def b_copy(to):
        return remote(out_b.at[to], in_b.at[mem], b_s, b_r, c - mem + to, hd)

    for to in mates:
        b_copy(to).start()
    in_b[mem] = out_b[mem]

    kv1_group(2)

    for p in (1, 2):
        x_copy(0, p).wait_recv()
    core_copy_own().start()

    def forward(d, carry):
        kv1_got(d).wait_recv()
        for p in range(3):
            x_copy(d, p).start()
        return carry

    lax.fori_loop(1, z + 1, forward, 0)

    remote(out_b.at[three], in_b.at[three], b_s, b_r, c, sib).wait_recv()
    entering = in_b[...].reshape(STATE, CHAN)
    squares = jnp.zeros((TOK, 128), F32)
    for part in range(2):
        cols = slice(part * 256, (part + 1) * 256)
        reach = jnp.dot(cb_v[...], entering[:, cols], preferred_element_type=F32)
        gated = (pre_v[:, cols] + ecx_v[:, cols] * reach) * sz_v[:, cols]
        pre_v[:, cols] = gated
        squares = squares + gated[:, :128] * gated[:, :128] + gated[:, 128:] * gated[:, 128:]
    sq_v[0] = jnp.sum(squares.T, axis=0, keepdims=True)

    def quad_copies():
        return [
            remote(sq_v.at[0], sq_v.at[1], q_s.at[0], q_r.at[0], c, sib),
            remote(sq_v.at[0], sq_v.at[2], q_s.at[1], q_r.at[1], c, hd + flip_l),
            remote(sq_v.at[0], sq_v.at[3], q_s.at[2], q_r.at[2], c, sib + flip_l),
        ]

    for cp in quad_copies():
        cp.start()
    kv1_group(3)

    def attend(keys, values, mask, first):
        logits = lax.dot_general(
            keys, q2_v[...], (((1,), (1,)), ((), ())), preferred_element_type=F32
        )
        if mask is not None:
            logits = jnp.where(mask, logits, NEGATIVE)
        top = jnp.max(logits, axis=0, keepdims=True)
        if not first:
            top = jnp.maximum(m_v[...], top)
        grown = jnp.exp2((logits - top) * EXP_SCALE)
        if mask is not None:
            grown = jnp.where(mask, grown, 0.0)
        den = jnp.sum(grown, axis=0, keepdims=True)
        got = jnp.dot(values.T, grown.astype(BF16), preferred_element_type=F32)
        if first:
            l_v[...] = den
            o_v[...] = got
        else:
            shrink = jnp.exp2((m_v[...] - top) * EXP_SCALE)
            l_v[...] = l_v[...] * shrink + den
            o_v[...] = o_v[...] * shrink + got
        m_v[...] = top

    load_q.wait()
    q2_v[0:TOK] = q_v[:, :HEAD_DIM]
    q2_v[TOK:] = q_v[:, HEAD_DIM:]
    key_at = lax.broadcasted_iota(jnp.int32, (TOK, 2 * TOK), 0)
    query_at = lax.rem(lax.broadcasted_iota(jnp.int32, (TOK, 2 * TOK), 1), TOK)
    attend(
        kvbuf[0, z, xh].reshape(TOK, HEAD_DIM), kvbuf[1, z, xh].reshape(TOK, HEAD_DIM),
        key_at <= query_at, True,
    )
    core_copy_own().wait_recv()

    @pl.when(xh == 1)
    def _():
        attend(
            kvbuf[0, z, 0].reshape(TOK, HEAD_DIM), kvbuf[1, z, 0].reshape(TOK, HEAD_DIM),
            None, False,
        )

    for cp in quad_copies():
        cp.wait_recv()
    group_total = sq_v[0] + sq_v[1] + sq_v[2] + sq_v[3]
    scale = lax.rsqrt(group_total * (1.0 / 2048.0) + EPSILON)
    scale_col = jnp.broadcast_to(scale, (8, TOK)).T[:, 0:1]
    ssm_v[...] = (pre_v[...] * scale_col * gain_ref[...]).astype(BF16)
    ssm_out = pltpu.make_async_copy(ssm_v, ssm_hbm, loc.at[12])
    ssm_out.start()

    def attend_row(d):
        core_copy(d).wait_recv()
        attend(
            kvbuf[0, z - d].reshape(2 * TOK, HEAD_DIM), kvbuf[1, z - d].reshape(2 * TOK, HEAD_DIM),
            None, False,
        )

    def to_core(d, carry):
        for p in range(3):
            x_copy(d, p).wait_recv()
        core_copy(d).start()

        @pl.when(d > 1)
        def _():
            attend_row(d - 1)

        return carry

    lax.fori_loop(1, z + 1, to_core, 0)

    @pl.when(z > 0)
    def _():
        attend_row(z)

    result = o_v[...] / l_v[...]
    for h in range(2):
        attn_v[:, h * HEAD_DIM : (h + 1) * HEAD_DIM] = result[
            :, h * TOK : (h + 1) * TOK
        ].T.astype(BF16)
    attn_out = pltpu.make_async_copy(attn_v, attn_hbm, loc.at[13])
    attn_out.start()

    @pl.when(c < N_CTX - 1)
    def _():
        for cp in halo_copies():
            cp.wait_send()

    remote(dec_in.at[three], dec_in.at[three], d_s, d_r, c, sib).wait_send()
    remote(st_send.at[three], in_a.at[three], a_s, a_r, c, sib).wait_send()
    remote(out_b.at[three], in_b.at[three], b_s, b_r, c, sib).wait_send()

    @pl.when(grp < 3)
    def _():
        e_copy().wait_send()

    def kv1_sent(d, carry):
        kv1_copy(d).wait_send()
        return carry

    lax.fori_loop(1, ROWS_Z - z, kv1_sent, 0)

    def row_sent(d, carry):
        for p in range(3):
            x_copy(d, p).wait_send()
        core_copy(d).wait_send()
        return carry

    lax.fori_loop(1, z + 1, row_sent, 0)
    for p in (1, 2):
        x_copy(0, p).wait_send()
    core_copy_own().wait_send()
    for cp in quad_copies():
        cp.wait_send()
    ssm_out.wait()
    attn_out.wait()


def hand_over(ssm_in, attn_in, ssm_ref, attn_ref, sems):
    copies = [
        pltpu.make_async_copy(ssm_in, ssm_ref, sems.at[0]),
        pltpu.make_async_copy(attn_in, attn_ref, sems.at[1]),
    ]
    for cp in copies:
        cp.start()
    for cp in copies:
        cp.wait()


def local(
    x_in, z_in, bc_in, dt_raw, a_log, d_skip, conv_x, conv_bc, norm_gain, queries, keys_values
):
    hbm = pl.BlockSpec(memory_space=pltpu.HBM)
    dma = pltpu.SemaphoreType.DMA
    out_shape = (
        jax.ShapeDtypeStruct((TOK, CHAN), BF16),
        jax.ShapeDtypeStruct((TOK, 2 * HEAD_DIM), BF16),
    )
    mixed = pl.pallas_call(
        kernel,
        out_shape=out_shape,
        in_specs=[hbm] * 11,
        out_specs=(hbm, hbm),
        scratch_shapes=[
            pltpu.VMEM((HEADS, TOK), F32),
            pltpu.SMEM((HEADS,), F32),
            pltpu.SMEM((HEADS,), F32),
            pltpu.VMEM((CONV, CHAN), BF16),
            pltpu.VMEM((CONV, 2 * GROUPS * STATE), BF16),
            pltpu.VMEM((1, CHAN), F32),
            pltpu.VMEM((TOK, CHAN), BF16),
            pltpu.VMEM((TOK, CHAN), BF16),
            pltpu.VMEM((TOK, STATE), BF16),
            pltpu.VMEM((TOK, STATE), BF16),
            pltpu.VMEM((TOK, 2 * HEAD_DIM), BF16),
            pltpu.VMEM((2 * TOK, HEAD_DIM), BF16),
            pltpu.VMEM((2, ROWS_Z, 2, 2, 2, QUART, HEAD_DIM), BF16),
            pltpu.VMEM((16, CHAN), BF16),
            pltpu.VMEM((2, 16, STATE), BF16),
            pltpu.VMEM((8 + TOK, CHAN), F32),
            pltpu.VMEM((8 + TOK, 2 * STATE), F32),
            pltpu.VMEM((TOK, STATE), F32),
            pltpu.VMEM((4, SLICE, CHAN), BF16),
            pltpu.VMEM((4, SLICE, CHAN), BF16),
            pltpu.VMEM((4, SLICE, CHAN), BF16),
            pltpu.VMEM((4, SLICE, CHAN), BF16),
            pltpu.VMEM((SLICE, CHAN), BF16),
            pltpu.VMEM((SLICE, CHAN), BF16),
            pltpu.VMEM((1, CHAN), F32),
            pltpu.VMEM((4, 1, CHAN), F32),
            pltpu.VMEM((TOK, CHAN), F32),
            pltpu.VMEM((TOK, CHAN), F32),
            pltpu.VMEM((TOK, CHAN), F32),
            pltpu.VMEM((TOK, STATE), BF16),
            pltpu.VMEM((4, 1, TOK), F32),
            pltpu.VMEM((1, 2 * TOK), F32),
            pltpu.VMEM((1, 2 * TOK), F32),
            pltpu.VMEM((HEAD_DIM, 2 * TOK), F32),
            pltpu.VMEM((TOK, CHAN), BF16),
            pltpu.VMEM((TOK, 2 * HEAD_DIM), BF16),
            dma((14,)), dma((3,)), dma((3,)),
            dma(()), dma(()), dma(()), dma(()), dma(()), dma(()), dma(()), dma(()),
            dma((3,)), dma((3,)), dma((ROWS_Z,)), dma((ROWS_Z,)),
            dma((ROWS_Z, 3)), dma((ROWS_Z, 3)), dma((ROWS_Z,)), dma((ROWS_Z,)),
            pltpu.SemaphoreType.REGULAR((3,)),
        ],
        compiler_params=pltpu.CompilerParams(
            collective_id=0, has_side_effects=True, vmem_limit_bytes=64 * 1024 * 1024
        ),
        name="mixer",
    )(
        x_in, z_in, bc_in, dt_raw, a_log, d_skip, conv_x, conv_bc,
        norm_gain.reshape(1, CHAN), queries,
        keys_values.reshape(2, 2, 2, QUART, GROUPS * HEAD_DIM),
    )
    return pl.pallas_call(
        hand_over,
        out_shape=out_shape,
        in_specs=[hbm, hbm],
        out_specs=(hbm, hbm),
        scratch_shapes=[dma((2,))],
        name="hand_over",
    )(*mixed)


def solution(mesh):
    placed = (
        P("ctx", "head"),
        P("ctx", "head"),
        P("ctx", None),
        P("head", "ctx"),
        P("head"),
        P("head"),
        P(None, "head"),
        P(),
        P("head"),
        P("ctx", "head"),
        P(None, "ctx", None),
    )
    return jax.shard_map(
        local,
        mesh=mesh,
        in_specs=placed,
        out_specs=(P("ctx", "head"), P("ctx", "head")),
        check_vma=False,
    )
```

```python
import functools
import math

import jax
import jax.numpy as jnp
from jax import lax
from jax.experimental import pallas as pl
from jax.experimental.pallas import tpu as pltpu
from jax.sharding import PartitionSpec as P

GROUPS = 8
STATE = 128
HEAD_DIM = 128
CONV = 4
TOK = 256
HEADS = 8
CHAN = 512
N_CTX = 16
BLOCK = 128
ROWS_Z = 8
SLICE = STATE // 8
QUART = TOK // 4
EPSILON = 1e-05
NEGATIVE = -1e30
HIGH = lax.Precision.HIGHEST
MESH = pl.DeviceIdType.MESH
F32 = jnp.float32
BF16 = jnp.bfloat16
PEERS = ((0, 1), (1, 0), (1, 1))
EXP_SCALE = math.log2(math.e) / math.sqrt(HEAD_DIM)


def silu(v):
    return v / (1.0 + jnp.exp(-v))


def conv_rows(pad_ref, taps, cols, rows):
    total = jnp.zeros((rows, cols.size), F32)
    for k in range(CONV):
        total = total + pad_ref[5 + k : 5 + k + rows, cols] * taps[k : k + 1]
    return silu(total)


def kernel(
    x_hbm, z_hbm, bc_hbm, dt_hbm, alog_hbm, dskip_hbm, cx_hbm, cbc_hbm, gain_hbm, q_hbm, kv_hbm,
    ssm_hbm, attn_hbm,
    dt_ref, alog_ref, dskip_ref, cx_ref, cbc_ref, gain_ref,
    x_v, z_v, b_v, c_v, q_v, q2_v, kvbuf, halo_x, halo_bc, pad_x, pad_bc, bf_v,
    st_send, in_a, out_b, in_b, e_out, e_in, dec_send, dec_in, pre_v, sz_v, ecx_v, cb_v, sq_v,
    m_v, l_v, o_v, ssm_v, attn_v,
    loc, h_s, h_r, d_s, d_r, a_s, a_r, b_s, b_r, e_s, e_r, q_s, q_r, s1_s, s1_r,
    x_s, x_r, c_s, c_r, rdy, rdy_e,
):
    c = lax.axis_index("ctx")
    hd = lax.axis_index("head")
    z, xh = lax.div(c, 2), lax.rem(c, 2)
    late = lax.div(c, 8)
    grp = lax.div(c, 4) - lax.div(c, 12)
    mem = (1 - late) * lax.rem(c, 4) + late * (c - 8)
    z_first = 2 * grp
    z_last = z_first + 1 + 2 * late
    y, qi = lax.div(hd, 4), lax.rem(hd, 4)
    xl, core = lax.div(qi, 2), lax.rem(qi, 2)
    flip_c = 1 - 2 * xh
    flip_l = 2 * (1 - 2 * xl)
    sib = hd + 1 - 2 * core
    ycol = pl.multiple_of(y * 128, 128)
    ycol2 = pl.multiple_of(GROUPS * STATE + y * 128, 128)

    def for_group(act):
        @pl.when(late == 0)
        def _():
            act(4, 2, [lax.rem(mem + e, 4) for e in range(1, 4)])

        @pl.when(late == 1)
        def _():
            act(8, 1, [lax.rem(mem + e, 8) for e in range(1, 8)])

    def remote(src, dst, ss, rs, ctx, head):
        return pltpu.make_async_remote_copy(
            src_ref=src, dst_ref=dst, send_sem=ss, recv_sem=rs,
            device_id=(ctx, head), device_id_type=MESH,
        )

    small = [
        pltpu.make_async_copy(src, dst, loc.at[i])
        for i, (src, dst) in enumerate(
            (
                (dt_hbm, dt_ref), (alog_hbm, alog_ref), (dskip_hbm, dskip_ref),
                (cx_hbm, cx_ref), (cbc_hbm, cbc_ref), (gain_hbm, gain_ref),
            )
        )
    ]
    load_x = pltpu.make_async_copy(x_hbm, x_v, loc.at[6])
    load_b = pltpu.make_async_copy(bc_hbm.at[:, pl.ds(ycol, 128)], b_v, loc.at[7])
    load_c = pltpu.make_async_copy(bc_hbm.at[:, pl.ds(ycol2, 128)], c_v, loc.at[8])
    load_q = pltpu.make_async_copy(q_hbm, q_v, loc.at[9])
    load_z = pltpu.make_async_copy(z_hbm, z_v, loc.at[10])
    load_kv = pltpu.make_async_copy(
        kv_hbm.at[:, :, :, :, pl.ds(ycol, 128)], kvbuf.at[:, z, xh], loc.at[11]
    )
    for cp in small + [load_b, load_c, load_x, load_kv, load_q, load_z]:
        cp.start()

    barrier = pltpu.get_barrier_semaphore()

    def greet(ctx, head):
        pl.semaphore_signal(barrier, inc=1, device_id=(ctx, head), device_id_type=MESH)

    def greet_mates(size, each, mates):
        for to in mates:
            greet(c - mem + to, hd)

    for_group(greet_mates)
    greet(c, sib)
    greet(c, hd + flip_l)
    greet(c, sib + flip_l)
    greet(c + flip_c, hd + flip_l)

    @pl.when((mem == 0) & (c > 0))
    def _():
        greet(c - 1, hd)

    @pl.when(grp == 1)
    def _():
        for k in range(2):
            greet(8 + 2 * mem + k, hd)

    def greet_later(d, carry):
        greet(c + 2 * d, hd)
        return carry

    lax.fori_loop(z_last + 1 - z, ROWS_Z - z, greet_later, 0)

    for cp in small:
        cp.wait()
    a_log = jnp.zeros((HEADS, 1), F32)
    head_row = lax.broadcasted_iota(jnp.int32, (HEADS, 1), 0)
    for h in range(HEADS):
        a_log = jnp.where(head_row == h, alog_ref[h], a_log)
    step = jnp.log(1.0 + jnp.exp(dt_ref[...]))
    cum = -jnp.exp(a_log) * step
    lane = lax.broadcasted_iota(jnp.int32, (HEADS, TOK), 1)
    shift = 1
    while shift < TOK:
        cum = cum + jnp.where(lane >= shift, pltpu.roll(cum, shift, 1), 0.0)
        shift *= 2
    last = cum[:, TOK - 1 : TOK]
    of_head = (
        lax.div(lax.broadcasted_iota(jnp.int32, (HEADS, CHAN), 1), CHAN // HEADS)
        == lax.broadcasted_iota(jnp.int32, (HEADS, CHAN), 0)
    )
    spread = jnp.where(of_head, 1.0, 0.0).astype(F32)
    dec_send[...] = jnp.sum(jnp.where(of_head, last, 0.0), axis=0, keepdims=True)
    dec_in[mem] = dec_send[...]
    tail = jnp.exp(last - cum) * step
    tail_x = jnp.dot(tail.T, spread, precision=HIGH, preferred_element_type=F32)

    greeted = 3 + 4 * late + 4 + 2 * grp + late + jnp.where((mem == 3) & (late == 0), 1, 0)
    pl.semaphore_wait(barrier, greeted)

    def halo_copies():
        tail_rows = pl.ds(TOK - 16, 16)
        return [
            remote(x_hbm.at[tail_rows, :], halo_x, h_s.at[0], h_r.at[0], c + 1, hd),
            remote(
                bc_hbm.at[tail_rows, pl.ds(ycol, 128)], halo_bc.at[0],
                h_s.at[1], h_r.at[1], c + 1, hd,
            ),
            remote(
                bc_hbm.at[tail_rows, pl.ds(ycol2, 128)], halo_bc.at[1],
                h_s.at[2], h_r.at[2], c + 1, hd,
            ),
        ]

    @pl.when(c < N_CTX - 1)
    def _():
        for cp in halo_copies():
            cp.start()

    def dec_copy(to):
        return remote(dec_send, dec_in.at[mem], d_s, d_r, c - mem + to, hd)

    def dec_start(size, each, mates):
        for to in mates:
            dec_copy(to).start()

    for_group(dec_start)

    def say_ready(sem, ctx):
        pl.semaphore_signal(sem, inc=1, device_id=(ctx, hd), device_id_type=MESH)

    @pl.when(grp == 1)
    def _():
        for row in range(2):
            say_ready(rdy.at[0], 2 * row + xh)

    @pl.when(grp == 2)
    def _():
        for row in range(4):
            say_ready(rdy.at[1], 2 * row + xh)
        say_ready(rdy_e, 4 + lax.div(mem, 2))

    def kv1_copy(d):
        return remote(
            kvbuf.at[:, z, xh, xl, core], kvbuf.at[:, z, xh, xl, core],
            s1_s.at[d], s1_r.at[d], c + 2 * d, hd,
        )

    def kv1_got(d):
        piece = kvbuf.at[:, z - d, xh, xl, core]
        return remote(piece, piece, s1_s.at[d], s1_r.at[d], c, sib)

    def kv1_start(d, carry):
        kv1_copy(d).start()
        return carry

    def kv1_group(grps, to_grp):
        @pl.when((grp >= grps[0]) & (grp <= grps[-1]))
        def _():
            rows = 2 * to_grp
            pl.semaphore_wait(rdy.at[to_grp - 1], rows)
            for row in range(rows):
                kv1_copy(rows + row - z).start()

    def x_copy(d, p):
        fh, fl = PEERS[p]
        piece = kvbuf.at[:, z - d, xh, xl, core]
        return remote(piece, piece, x_s.at[d, p], x_r.at[d, p], c + fh * flip_c, hd + fl * flip_l)

    def core_copy(d):
        piece = kvbuf.at[:, z - d, :, :, core]
        return remote(piece, piece, c_s.at[d], c_r.at[d], c, sib)

    def core_copy_own():
        piece = kvbuf.at[:, z, 1 - xh, :, core]
        return remote(piece, piece, c_s.at[0], c_r.at[0], c, sib)

    load_kv.wait()
    for p in (1, 2):
        x_copy(0, p).start()
    lax.fori_loop(1, z_last + 1 - z, kv1_start, 0)

    taps_b = cbc_ref[:, pl.ds(ycol, 128)].astype(F32)
    taps_c = cbc_ref[:, pl.ds(ycol2, 128)].astype(F32)
    taps_x = cx_ref[...].astype(F32)
    pad_bc[0:8] = jnp.zeros((8, 2 * STATE), F32)
    pad_x[0:8] = jnp.zeros((8, CHAN), F32)
    load_b.wait()
    load_c.wait()
    pad_bc[8:, 0:STATE] = b_v[...].astype(F32)
    pad_bc[8:, STATE:] = c_v[...].astype(F32)

    def convolve(rows):
        bf_v[0:rows] = conv_rows(pad_bc, taps_b, pl.ds(0, STATE), rows)
        cb_v[0:rows] = conv_rows(pad_bc, taps_c, pl.ds(STATE, STATE), rows).astype(BF16)
        x_v[0:rows] = conv_rows(pad_x, taps_x, pl.ds(0, CHAN), rows).astype(BF16)

    load_x.wait()
    pad_x[8:] = x_v[...].astype(F32)
    convolve(TOK)

    @pl.when(c > 0)
    def _():
        for cp in halo_copies():
            cp.wait_recv()
        pad_bc[0:8, 0:STATE] = halo_bc[0].astype(F32)[8:16]
        pad_bc[0:8, STATE:] = halo_bc[1].astype(F32)[8:16]
        pad_x[0:8] = halo_x[...].astype(F32)[8:16]
        convolve(16)

    b_t = bf_v[...].T.astype(BF16)
    carried = (tail_x * x_v[...].astype(F32)).astype(BF16)
    state = jnp.dot(b_t, carried, preferred_element_type=F32).astype(BF16)
    st_send[...] = state.reshape(8, SLICE, CHAN)

    def a_start(size, each, mates):
        for to in mates:
            remote(
                st_send.at[pl.ds(each * to, each)], in_a.at[mem, pl.ds(0, each)],
                a_s, a_r, c - mem + to, hd,
            ).start()
        in_a[mem, 0:each] = st_send[pl.ds(each * mem, each)]

    def a_all(size, each):
        some = pl.ds(0, (size - 1) * each)
        return remote(st_send.at[some], st_send.at[some], a_s, a_r, c, sib)

    for_group(a_start)
    kv1_group((0,), 1)

    scores = jnp.dot(cb_v[...], b_t, preferred_element_type=F32)
    t_at = lax.broadcasted_iota(jnp.int32, (TOK, TOK), 0)
    s_at = lax.broadcasted_iota(jnp.int32, (TOK, TOK), 1)
    scores = jnp.where(s_at <= t_at, scores, 0.0)
    cum_t = cum.T
    skip_row = jnp.zeros((1, CHAN), F32)
    head_of_lane = lax.div(lax.broadcasted_iota(jnp.int32, (1, CHAN), 1), CHAN // HEADS)
    for h in range(HEADS):
        skip_row = jnp.where(head_of_lane == h, dskip_ref[h], skip_row)
    left = lax.broadcasted_iota(jnp.int32, (BLOCK, 128), 1) < 64
    for low in (0, BLOCK):
        rows, upto = slice(low, low + BLOCK), low + BLOCK
        for pair in range(HEADS // 2):
            cols = slice(128 * pair, 128 * pair + 128)
            both = []
            for h in (2 * pair, 2 * pair + 1):
                gap = jnp.minimum(cum_t[rows, h : h + 1] - cum[h : h + 1, :upto], 0.0)
                weights = (scores[rows, :upto] * jnp.exp(gap) * step[h : h + 1, :upto]).astype(BF16)
                both.append(jnp.dot(weights, x_v[:upto, cols], preferred_element_type=F32))
            pre_v[rows, cols] = (
                jnp.where(left, both[0], both[1])
                + skip_row[:, cols] * x_v[rows, cols].astype(F32)
            )
    ecx_v[...] = jnp.dot(jnp.exp(cum).T, spread, precision=HIGH, preferred_element_type=F32)
    load_z.wait()
    sz_v[...] = silu(z_v[...].astype(F32))

    kv1_group((1,), 2)
    for p in (1, 2):
        x_copy(0, p).wait_recv()
    core_copy_own().start()

    def forward(d, carry):
        kv1_got(d).wait_recv()
        for p in range(3):
            x_copy(d, p).start()
        return carry

    near = z - z_first + 1
    lax.fori_loop(1, near, forward, 0)

    def dec_all(size):
        some = pl.ds(0, size - 1)
        return remote(dec_in.at[some], dec_in.at[some], d_s, d_r, c, sib)

    def e_copies(number):
        if number == 0:
            return [remote(e_out, e_in, e_s, e_r, c + 4, hd)]
        return [
            remote(e_out.at[pl.ds(k, 1)], e_in.at[pl.ds(0, 1)], e_s, e_r, 8 + 2 * mem + k, hd)
            for k in range(2)
        ]

    def scan(size, each, mates):
        dec_all(size).wait_recv()
        a_all(size, each).wait_recv()
        part = pl.ds(0, each)
        if size == 8:
            remote(e_in.at[part], e_in.at[part], e_s, e_r, c, sib).wait_recv()
        else:

            @pl.when(grp == 1)
            def _():
                remote(e_in, e_in, e_s, e_r, c, sib).wait_recv()

            @pl.when(grp == 0)
            def _():
                e_in[...] = jnp.zeros_like(e_in)

        running = e_in[0:each].astype(F32)
        for k in range(size):
            out_b[k, 0:each] = running.astype(BF16)
            running = jnp.exp(dec_in[k]) * running + in_a[k, 0:each].astype(F32)
        if size == 4:
            e_out[...] = running.astype(BF16)

            @pl.when(grp == 0)
            def _():
                for cp in e_copies(0):
                    cp.start()

            @pl.when(grp == 1)
            def _():
                pl.semaphore_wait(rdy_e, 2)
                for cp in e_copies(1):
                    cp.start()

        for to in mates:
            remote(
                out_b.at[to, part], in_b.at[pl.ds(each * mem, each)],
                b_s, b_r, c - mem + to, hd,
            ).start()
        in_b[pl.ds(each * mem, each)] = out_b[mem, 0:each]

    for_group(scan)
    kv1_group((0,), 2)
    lax.fori_loop(near, z + 1, forward, 0)

    def attend(keys, values, mask, first):
        logits = lax.dot_general(
            keys, q2_v[...], (((1,), (1,)), ((), ())), preferred_element_type=F32
        )
        if mask is not None:
            logits = jnp.where(mask, logits, NEGATIVE)
        top = jnp.max(logits, axis=0, keepdims=True)
        if not first:
            top = jnp.maximum(m_v[...], top)
        grown = jnp.exp2((logits - top) * EXP_SCALE)
        if mask is not None:
            grown = jnp.where(mask, grown, 0.0)
        den = jnp.sum(grown, axis=0, keepdims=True)
        got = jnp.dot(values.T, grown.astype(BF16), preferred_element_type=F32)
        if first:
            l_v[...] = den
            o_v[...] = got
        else:
            shrink = jnp.exp2((m_v[...] - top) * EXP_SCALE)
            l_v[...] = l_v[...] * shrink + den
            o_v[...] = o_v[...] * shrink + got
        m_v[...] = top

    load_q.wait()
    q2_v[0:TOK] = q_v[:, :HEAD_DIM]
    q2_v[TOK:] = q_v[:, HEAD_DIM:]
    key_at = lax.broadcasted_iota(jnp.int32, (TOK, 2 * TOK), 0)
    query_at = lax.rem(lax.broadcasted_iota(jnp.int32, (TOK, 2 * TOK), 1), TOK)
    attend(
        kvbuf[0, z, xh].reshape(TOK, HEAD_DIM), kvbuf[1, z, xh].reshape(TOK, HEAD_DIM),
        key_at <= query_at, True,
    )
    core_copy_own().wait_recv()

    @pl.when(xh == 1)
    def _():
        attend(
            kvbuf[0, z, 0].reshape(TOK, HEAD_DIM), kvbuf[1, z, 0].reshape(TOK, HEAD_DIM),
            None, False,
        )

    def to_core(d, carry):
        for p in range(3):
            x_copy(d, p).wait_recv()
        core_copy(d).start()
        return carry

    lax.fori_loop(1, near, to_core, 0)

    def b_all(size, each):
        some = pl.ds(0, (size - 1) * each)
        return remote(in_b.at[some], in_b.at[some], b_s, b_r, c, sib)

    for_group(lambda size, each, mates: b_all(size, each).wait_recv())
    entering = in_b[...].reshape(STATE, CHAN)
    squares = jnp.zeros((TOK, 128), F32)
    for part in range(2):
        cols = slice(part * 256, (part + 1) * 256)
        reach = jnp.dot(cb_v[...], entering[:, cols], preferred_element_type=F32)
        gated = (pre_v[:, cols] + ecx_v[:, cols] * reach) * sz_v[:, cols]
        pre_v[:, cols] = gated
        squares = squares + gated[:, :128] * gated[:, :128] + gated[:, 128:] * gated[:, 128:]
    sq_v[0] = jnp.sum(squares.T, axis=0, keepdims=True)

    def quad_copies():
        return [
            remote(sq_v.at[0], sq_v.at[1], q_s.at[0], q_r.at[0], c, sib),
            remote(sq_v.at[0], sq_v.at[2], q_s.at[1], q_r.at[1], c, hd + flip_l),
            remote(sq_v.at[0], sq_v.at[3], q_s.at[2], q_r.at[2], c, sib + flip_l),
        ]

    for cp in quad_copies():
        cp.start()

    def attend_row(d):
        core_copy(d).wait_recv()
        attend(
            kvbuf[0, z - d].reshape(2 * TOK, HEAD_DIM), kvbuf[1, z - d].reshape(2 * TOK, HEAD_DIM),
            None, False,
        )

    def one_row(d, carry):
        @pl.when(d >= near)
        def _():
            to_core(d, 0)

        @pl.when(d > 1)
        def _():
            attend_row(d - 1)

        return carry

    lax.fori_loop(1, z + 1, one_row, 0)

    @pl.when(z > 0)
    def _():
        attend_row(z)

    result = o_v[...] / l_v[...]
    for h in range(2):
        attn_v[:, h * HEAD_DIM : (h + 1) * HEAD_DIM] = result[
            :, h * TOK : (h + 1) * TOK
        ].T.astype(BF16)
    attn_out = pltpu.make_async_copy(attn_v, attn_hbm, loc.at[13])
    attn_out.start()

    for cp in quad_copies():
        cp.wait_recv()
    group_total = sq_v[0] + sq_v[1] + sq_v[2] + sq_v[3]
    scale = lax.rsqrt(group_total * (1.0 / 2048.0) + EPSILON)
    scale_col = jnp.broadcast_to(scale, (8, TOK)).T[:, 0:1]
    ssm_v[...] = (pre_v[...] * scale_col * gain_ref[...]).astype(BF16)
    ssm_out = pltpu.make_async_copy(ssm_v, ssm_hbm, loc.at[12])
    ssm_out.start()

    @pl.when(c < N_CTX - 1)
    def _():
        for cp in halo_copies():
            cp.wait_send()

    def group_sent(size, each, mates):
        dec_all(size).wait_send()
        a_all(size, each).wait_send()
        b_all(size, each).wait_send()

    for_group(group_sent)

    @pl.when(grp < 2)
    def _():
        remote(e_out, e_in, e_s, e_r, c, sib).wait_send()

    def kv1_sent(d, carry):
        kv1_copy(d).wait_send()
        return carry

    lax.fori_loop(1, ROWS_Z - z, kv1_sent, 0)

    def row_sent(d, carry):
        for p in range(3):
            x_copy(d, p).wait_send()
        core_copy(d).wait_send()
        return carry

    lax.fori_loop(1, z + 1, row_sent, 0)
    for p in (1, 2):
        x_copy(0, p).wait_send()
    core_copy_own().wait_send()
    for cp in quad_copies():
        cp.wait_send()
    ssm_out.wait()
    attn_out.wait()


def hand_over(ssm_in, attn_in, ssm_ref, attn_ref, ssm_v, attn_v, sems):
    into = [
        pltpu.make_async_copy(ssm_in, ssm_v, sems.at[0]),
        pltpu.make_async_copy(attn_in, attn_v, sems.at[1]),
    ]
    out = [
        pltpu.make_async_copy(ssm_v, ssm_ref, sems.at[2]),
        pltpu.make_async_copy(attn_v, attn_ref, sems.at[3]),
    ]
    for cp in into:
        cp.start()
    for cp, later in zip(into, out):
        cp.wait()
        later.start()
    for cp in out:
        cp.wait()


def local(
    x_in, z_in, bc_in, dt_raw, a_log, d_skip, conv_x, conv_bc, norm_gain, queries, keys_values
):
    hbm = pl.BlockSpec(memory_space=pltpu.HBM)
    dma = pltpu.SemaphoreType.DMA
    out_shape = (
        jax.ShapeDtypeStruct((TOK, CHAN), BF16),
        jax.ShapeDtypeStruct((TOK, 2 * HEAD_DIM), BF16),
    )
    mixed = pl.pallas_call(
        kernel,
        out_shape=out_shape,
        in_specs=[hbm] * 11,
        out_specs=(hbm, hbm),
        scratch_shapes=[
            pltpu.VMEM((HEADS, TOK), F32),
            pltpu.SMEM((HEADS,), F32),
            pltpu.SMEM((HEADS,), F32),
            pltpu.VMEM((CONV, CHAN), BF16),
            pltpu.VMEM((CONV, 2 * GROUPS * STATE), BF16),
            pltpu.VMEM((1, CHAN), F32),
            pltpu.VMEM((TOK, CHAN), BF16),
            pltpu.VMEM((TOK, CHAN), BF16),
            pltpu.VMEM((TOK, STATE), BF16),
            pltpu.VMEM((TOK, STATE), BF16),
            pltpu.VMEM((TOK, 2 * HEAD_DIM), BF16),
            pltpu.VMEM((2 * TOK, HEAD_DIM), BF16),
            pltpu.VMEM((2, ROWS_Z, 2, 2, 2, QUART, HEAD_DIM), BF16),
            pltpu.VMEM((16, CHAN), BF16),
            pltpu.VMEM((2, 16, STATE), BF16),
            pltpu.VMEM((8 + TOK, CHAN), F32),
            pltpu.VMEM((8 + TOK, 2 * STATE), F32),
            pltpu.VMEM((TOK, STATE), F32),
            pltpu.VMEM((8, SLICE, CHAN), BF16),
            pltpu.VMEM((8, 2, SLICE, CHAN), BF16),
            pltpu.VMEM((8, 2, SLICE, CHAN), BF16),
            pltpu.VMEM((8, SLICE, CHAN), BF16),
            pltpu.VMEM((2, SLICE, CHAN), BF16),
            pltpu.VMEM((2, SLICE, CHAN), BF16),
            pltpu.VMEM((1, CHAN), F32),
            pltpu.VMEM((8, 1, CHAN), F32),
            pltpu.VMEM((TOK, CHAN), F32),
            pltpu.VMEM((TOK, CHAN), F32),
            pltpu.VMEM((TOK, CHAN), F32),
            pltpu.VMEM((TOK, STATE), BF16),
            pltpu.VMEM((4, 1, TOK), F32),
            pltpu.VMEM((1, 2 * TOK), F32),
            pltpu.VMEM((1, 2 * TOK), F32),
            pltpu.VMEM((HEAD_DIM, 2 * TOK), F32),
            pltpu.VMEM((TOK, CHAN), BF16),
            pltpu.VMEM((TOK, 2 * HEAD_DIM), BF16),
            dma((14,)), dma((3,)), dma((3,)),
            dma(()), dma(()), dma(()), dma(()), dma(()), dma(()), dma(()), dma(()),
            dma((3,)), dma((3,)), dma((ROWS_Z,)), dma((ROWS_Z,)),
            dma((ROWS_Z, 3)), dma((ROWS_Z, 3)), dma((ROWS_Z,)), dma((ROWS_Z,)),
            pltpu.SemaphoreType.REGULAR((2,)),
            pltpu.SemaphoreType.REGULAR,
        ],
        compiler_params=pltpu.CompilerParams(
            collective_id=0, has_side_effects=True, vmem_limit_bytes=64 * 1024 * 1024
        ),
        name="mixer",
    )(
        x_in, z_in, bc_in, dt_raw, a_log, d_skip, conv_x, conv_bc,
        norm_gain.reshape(1, CHAN), queries,
        keys_values.reshape(2, 2, 2, QUART, GROUPS * HEAD_DIM),
    )
    return pl.pallas_call(
        hand_over,
        out_shape=out_shape,
        in_specs=[hbm, hbm],
        out_specs=(hbm, hbm),
        scratch_shapes=[
            pltpu.VMEM((TOK, CHAN), BF16), pltpu.VMEM((TOK, 2 * HEAD_DIM), BF16), dma((4,)),
        ],
        name="hand_over",
    )(*mixed)


def solution(mesh):
    placed = (
        P("ctx", "head"),
        P("ctx", "head"),
        P("ctx", None),
        P("head", "ctx"),
        P("head"),
        P("head"),
        P(None, "head"),
        P(),
        P("head"),
        P("ctx", "head"),
        P(None, "ctx", None),
    )
    return jax.shard_map(
        local,
        mesh=mesh,
        in_specs=placed,
        out_specs=(P("ctx", "head"), P("ctx", "head")),
        check_vma=False,
    )
```

```python
import functools
import math

import jax
import jax.numpy as jnp
from jax import lax
from jax.experimental import pallas as pl
from jax.experimental.pallas import tpu as pltpu
from jax.sharding import PartitionSpec as P

GROUPS = 8
STATE = 128
HEAD_DIM = 128
CONV = 4
TOK = 256
HEADS = 8
CHAN = 512
N_CTX = 16
BLOCK = 128
ROWS_Z = 8
SLICE = STATE // 8
QUART = TOK // 4
EPSILON = 1e-05
NEGATIVE = -1e30
HIGH = lax.Precision.HIGHEST
MESH = pl.DeviceIdType.MESH
F32 = jnp.float32
BF16 = jnp.bfloat16
PEERS = ((0, 1), (1, 0), (1, 1))
EXP_SCALE = math.log2(math.e) / math.sqrt(HEAD_DIM)


def silu(v):
    return v / (1.0 + jnp.exp(-v))


def conv_rows(pad_ref, taps, cols, rows):
    total = jnp.zeros((rows, cols.size), F32)
    for k in range(CONV):
        total = total + pad_ref[5 + k : 5 + k + rows, cols] * taps[k : k + 1]
    return silu(total)


def kernel(
    x_hbm, z_hbm, bc_hbm, dt_hbm, alog_hbm, dskip_hbm, cx_hbm, cbc_hbm, gain_hbm, q_hbm, kv_hbm,
    ssm_hbm, attn_hbm,
    dt_ref, alog_ref, dskip_ref, cx_ref, cbc_ref, gain_ref,
    x_v, z_v, b_v, c_v, q_v, q2_v, kvbuf, halo_x, halo_bc, pad_x, pad_bc, bf_v,
    st_send, in_a, out_b, in_b, e_out, e_in, t_in, lt_out, lt_in, dec_send, dec_in, pre_v, sz_v, ecx_v, cb_v, sq_v,
    m_v, l_v, o_v, ssm_v, attn_v,
    loc, h_s, h_r, d_s, d_r, a_s, a_r, b_s, b_r, e_s, e_r, f_s, f_r, t_s, t_r, lt_s, lt_r, q_s, q_r, s1_s, s1_r,
    x_s, x_r, c_s, c_r, rdy, rdy_e, r_s,
):
    c = lax.axis_index("ctx")
    hd = lax.axis_index("head")
    z, xh = lax.div(c, 2), lax.rem(c, 2)
    late = lax.div(c, 8)
    grp = lax.div(c, 4) - lax.div(c, 12)
    mem = (1 - late) * lax.rem(c, 4) + late * (c - 8)
    z_first = 2 * grp
    z_last = z_first + 1 + 2 * late
    y, qi = lax.div(hd, 4), lax.rem(hd, 4)
    xl, core = lax.div(qi, 2), lax.rem(qi, 2)
    flip_c = 1 - 2 * xh
    flip_l = 2 * (1 - 2 * xl)
    sib = hd + 1 - 2 * core
    ycol = pl.multiple_of(y * 128, 128)
    ycol2 = pl.multiple_of(GROUPS * STATE + y * 128, 128)

    def for_group(act):
        @pl.when(late == 0)
        def _():
            act(4, 2, [lax.rem(mem + e, 4) for e in range(1, 4)])

        @pl.when(late == 1)
        def _():
            act(8, 1, [lax.rem(mem + e, 8) for e in range(1, 8)])

    def remote(src, dst, ss, rs, ctx, head):
        return pltpu.make_async_remote_copy(
            src_ref=src, dst_ref=dst, send_sem=ss, recv_sem=rs,
            device_id=(ctx, head), device_id_type=MESH,
        )

    small = [
        pltpu.make_async_copy(src, dst, loc.at[i])
        for i, (src, dst) in enumerate(
            (
                (dt_hbm, dt_ref), (alog_hbm, alog_ref), (dskip_hbm, dskip_ref),
                (cx_hbm, cx_ref), (cbc_hbm, cbc_ref), (gain_hbm, gain_ref),
            )
        )
    ]
    load_x = pltpu.make_async_copy(x_hbm, x_v, loc.at[6])
    load_b = pltpu.make_async_copy(bc_hbm.at[:, pl.ds(ycol, 128)], b_v, loc.at[7])
    load_c = pltpu.make_async_copy(bc_hbm.at[:, pl.ds(ycol2, 128)], c_v, loc.at[8])
    load_q = pltpu.make_async_copy(q_hbm, q_v, loc.at[9])
    load_z = pltpu.make_async_copy(z_hbm, z_v, loc.at[10])
    load_kv = pltpu.make_async_copy(
        kv_hbm.at[:, :, :, :, pl.ds(ycol, 128)], kvbuf.at[:, z, xh], loc.at[11]
    )
    for cp in small + [load_b, load_c, load_x, load_kv, load_q, load_z]:
        cp.start()

    barrier = pltpu.get_barrier_semaphore()

    def greet(ctx, head):
        pl.semaphore_signal(barrier, inc=1, device_id=(ctx, head), device_id_type=MESH)

    def greet_mates(size, each, mates):
        for to in mates:
            greet(c - mem + to, hd)

    for_group(greet_mates)
    greet(c, sib)
    greet(c, hd + flip_l)
    greet(c, sib + flip_l)
    greet(c + flip_c, hd + flip_l)

    @pl.when((mem == 0) & (c > 0))
    def _():
        greet(c - 1, hd)

    @pl.when(grp < 2)
    def _():
        for k in range(2):
            greet(8 + 2 * mem + k, hd)

    @pl.when(grp == 0)
    def _():
        for row in (2, 3):
            greet(2 * row + xh, hd)

    @pl.when(grp < 2)
    def _():
        greet(c + 8, hd)

    for cp in small:
        cp.wait()
    a_log = jnp.zeros((HEADS, 1), F32)
    head_row = lax.broadcasted_iota(jnp.int32, (HEADS, 1), 0)
    for h in range(HEADS):
        a_log = jnp.where(head_row == h, alog_ref[h], a_log)
    step = jnp.log(1.0 + jnp.exp(dt_ref[...]))
    cum = -jnp.exp(a_log) * step
    lane = lax.broadcasted_iota(jnp.int32, (HEADS, TOK), 1)
    shift = 1
    while shift < TOK:
        cum = cum + jnp.where(lane >= shift, pltpu.roll(cum, shift, 1), 0.0)
        shift *= 2
    last = cum[:, TOK - 1 : TOK]
    of_head = (
        lax.div(lax.broadcasted_iota(jnp.int32, (HEADS, CHAN), 1), CHAN // HEADS)
        == lax.broadcasted_iota(jnp.int32, (HEADS, CHAN), 0)
    )
    spread = jnp.where(of_head, 1.0, 0.0).astype(F32)
    dec_send[...] = jnp.sum(jnp.where(of_head, last, 0.0), axis=0, keepdims=True)
    dec_in[mem] = dec_send[...]
    tail = jnp.exp(last - cum) * step
    tail_x = jnp.dot(tail.T, spread, precision=HIGH, preferred_element_type=F32)

    greeted = 3 + 4 * late + 4 + jnp.where(grp == 1, 2, 0) + 3 * late + jnp.where((mem == 3) & (late == 0), 1, 0)
    pl.semaphore_wait(barrier, greeted)

    def halo_copies():
        tail_rows = pl.ds(TOK - 16, 16)
        return [
            remote(x_hbm.at[tail_rows, :], halo_x, h_s.at[0], h_r.at[0], c + 1, hd),
            remote(
                bc_hbm.at[tail_rows, pl.ds(ycol, 128)], halo_bc.at[0],
                h_s.at[1], h_r.at[1], c + 1, hd,
            ),
            remote(
                bc_hbm.at[tail_rows, pl.ds(ycol2, 128)], halo_bc.at[1],
                h_s.at[2], h_r.at[2], c + 1, hd,
            ),
        ]

    @pl.when(c < N_CTX - 1)
    def _():
        for cp in halo_copies():
            cp.start()

    def say_ready(sem, ctx):
        pl.semaphore_signal(sem, inc=1, device_id=(ctx, hd), device_id_type=MESH)

    @pl.when(grp == 1)
    def _():
        for row in range(2):
            say_ready(rdy.at[0], 2 * row + xh)

    @pl.when(grp == 2)
    def _():
        say_ready(rdy.at[1], c - 8)
        say_ready(rdy_e, lax.div(mem, 2))
        say_ready(rdy_e, 4 + lax.div(mem, 2))

    def dec_copy(to):
        return remote(dec_send, dec_in.at[mem], d_s, d_r, c - mem + to, hd)

    def dec_start(size, each, mates):
        for to in mates:
            dec_copy(to).start()

    for_group(dec_start)

    def kv1_copy(d):
        return remote(
            kvbuf.at[:, z, xh, xl, core], kvbuf.at[:, z, xh, xl, core],
            s1_s.at[d], s1_r.at[d], c + 2 * d, hd,
        )

    def kv1_got(d):
        piece = kvbuf.at[:, z - d, xh, xl, core]
        return remote(piece, piece, s1_s.at[d], s1_r.at[d], c, sib)

    def kv1_start(d, carry):
        kv1_copy(d).start()
        return carry

    def kv1_next():
        pl.semaphore_wait(rdy.at[0], 2)
        for row in (2, 3):
            kv1_copy(row - z).start()

    def kv1_late():
        pl.semaphore_wait(rdy.at[1], 1)
        kv1_copy(4).start()

    def relay_copy(e):
        row = 4 + lax.rem(z - 4 + e, 4)
        piece = kvbuf.at[:, z - 4, xh, xl, core]
        return remote(piece, piece, r_s.at[e], s1_r.at[row + 4 - z], 2 * row + xh, hd)

    def x_copy(d, p):
        fh, fl = PEERS[p]
        piece = kvbuf.at[:, z - d, xh, xl, core]
        return remote(piece, piece, x_s.at[d, p], x_r.at[d, p], c + fh * flip_c, hd + fl * flip_l)

    def core_copy(d):
        piece = kvbuf.at[:, z - d, :, :, core]
        return remote(piece, piece, c_s.at[d], c_r.at[d], c, sib)

    def core_copy_own():
        piece = kvbuf.at[:, z, 1 - xh, :, core]
        return remote(piece, piece, c_s.at[0], c_r.at[0], c, sib)

    load_kv.wait()
    for p in (1, 2):
        x_copy(0, p).start()
    lax.fori_loop(1, z_last + 1 - z, kv1_start, 0)

    taps_b = cbc_ref[:, pl.ds(ycol, 128)].astype(F32)
    taps_c = cbc_ref[:, pl.ds(ycol2, 128)].astype(F32)
    taps_x = cx_ref[...].astype(F32)
    pad_bc[0:8] = jnp.zeros((8, 2 * STATE), F32)
    pad_x[0:8] = jnp.zeros((8, CHAN), F32)
    load_b.wait()
    load_c.wait()
    pad_bc[8:, 0:STATE] = b_v[...].astype(F32)
    pad_bc[8:, STATE:] = c_v[...].astype(F32)

    def convolve(rows):
        bf_v[0:rows] = conv_rows(pad_bc, taps_b, pl.ds(0, STATE), rows)
        cb_v[0:rows] = conv_rows(pad_bc, taps_c, pl.ds(STATE, STATE), rows).astype(BF16)
        x_v[0:rows] = conv_rows(pad_x, taps_x, pl.ds(0, CHAN), rows).astype(BF16)

    load_x.wait()
    pad_x[8:] = x_v[...].astype(F32)
    convolve(TOK)

    def attend(keys, values, mask, first):
        logits = lax.dot_general(
            keys, q2_v[...], (((1,), (1,)), ((), ())), preferred_element_type=F32
        )
        if mask is not None:
            logits = jnp.where(mask, logits, NEGATIVE)
        top = jnp.max(logits, axis=0, keepdims=True)
        if not first:
            top = jnp.maximum(m_v[...], top)
        grown = jnp.exp2((logits - top) * EXP_SCALE)
        if mask is not None:
            grown = jnp.where(mask, grown, 0.0)
        den = jnp.sum(grown, axis=0, keepdims=True)
        got = jnp.dot(values.T, grown.astype(BF16), preferred_element_type=F32)
        if first:
            l_v[...] = den
            o_v[...] = got
        else:
            shrink = jnp.exp2((m_v[...] - top) * EXP_SCALE)
            l_v[...] = l_v[...] * shrink + den
            o_v[...] = o_v[...] * shrink + got
        m_v[...] = top

    load_q.wait()
    q2_v[0:TOK] = q_v[:, :HEAD_DIM]
    q2_v[TOK:] = q_v[:, HEAD_DIM:]
    key_at = lax.broadcasted_iota(jnp.int32, (TOK, 2 * TOK), 0)
    query_at = lax.rem(lax.broadcasted_iota(jnp.int32, (TOK, 2 * TOK), 1), TOK)
    attend(
        kvbuf[0, z, xh].reshape(TOK, HEAD_DIM), kvbuf[1, z, xh].reshape(TOK, HEAD_DIM),
        key_at <= query_at, True,
    )
    @pl.when(c > 0)
    def _():
        for cp in halo_copies():
            cp.wait_recv()
        pad_bc[0:8, 0:STATE] = halo_bc[0].astype(F32)[8:16]
        pad_bc[0:8, STATE:] = halo_bc[1].astype(F32)[8:16]
        pad_x[0:8] = halo_x[...].astype(F32)[8:16]
        convolve(16)

    b_t = bf_v[...].T.astype(BF16)
    carried = (tail_x * x_v[...].astype(F32)).astype(BF16)
    state = jnp.dot(b_t, carried, preferred_element_type=F32).astype(BF16)
    st_send[...] = state.reshape(8, SLICE, CHAN)

    def a_start(size, each, mates):
        for to in mates:
            remote(
                st_send.at[pl.ds(each * to, each)], in_a.at[mem, pl.ds(0, each)],
                a_s, a_r, c - mem + to, hd,
            ).start()
        in_a[mem, 0:each] = st_send[pl.ds(each * mem, each)]

    def a_all(size, each):
        some = pl.ds(0, (size - 1) * each)
        return remote(st_send.at[some], st_send.at[some], a_s, a_r, c, sib)

    for_group(a_start)

    @pl.when(grp == 0)
    def _():
        kv1_next()


    scores = jnp.dot(cb_v[...], b_t, preferred_element_type=F32)
    t_at = lax.broadcasted_iota(jnp.int32, (TOK, TOK), 0)
    s_at = lax.broadcasted_iota(jnp.int32, (TOK, TOK), 1)
    scores = jnp.where(s_at <= t_at, scores, 0.0)
    cum_t = cum.T
    skip_row = jnp.zeros((1, CHAN), F32)
    head_of_lane = lax.div(lax.broadcasted_iota(jnp.int32, (1, CHAN), 1), CHAN // HEADS)
    for h in range(HEADS):
        skip_row = jnp.where(head_of_lane == h, dskip_ref[h], skip_row)
    left = lax.broadcasted_iota(jnp.int32, (BLOCK, 128), 1) < 64
    for low in (0, BLOCK):
        rows, upto = slice(low, low + BLOCK), low + BLOCK
        for pair in range(HEADS // 2):
            cols = slice(128 * pair, 128 * pair + 128)
            both = []
            for h in (2 * pair, 2 * pair + 1):
                gap = jnp.minimum(cum_t[rows, h : h + 1] - cum[h : h + 1, :upto], 0.0)
                weights = (scores[rows, :upto] * jnp.exp(gap) * step[h : h + 1, :upto]).astype(BF16)
                both.append(jnp.dot(weights, x_v[:upto, cols], preferred_element_type=F32))
            pre_v[rows, cols] = (
                jnp.where(left, both[0], both[1])
                + skip_row[:, cols] * x_v[rows, cols].astype(F32)
            )
    ecx_v[...] = jnp.dot(jnp.exp(cum).T, spread, precision=HIGH, preferred_element_type=F32)
    load_z.wait()
    sz_v[...] = silu(z_v[...].astype(F32))

    @pl.when(grp == 1)
    def _():
        kv1_late()

    for p in (1, 2):
        x_copy(0, p).wait_recv()
    core_copy_own().start()

    def forward(d, carry):
        kv1_got(d).wait_recv()
        for p in range(3):
            x_copy(d, p).start()
        return carry

    near = z - z_first + 1
    lax.fori_loop(1, near, forward, 0)

    @pl.when(late == 1)
    def _():
        kv1_got(4).wait_recv()
        for e in range(1, 4):
            relay_copy(e).start()
        for p in range(3):
            x_copy(4, p).start()

    def dec_all(size):
        some = pl.ds(0, size - 1)
        return remote(dec_in.at[some], dec_in.at[some], d_s, d_r, c, sib)

    one = pl.ds(0, 1)

    def e_copy():
        return remote(e_out, e_in, e_s, e_r, c + 4, hd)

    def to_late(src, dst, sem, got):
        return [remote(src(k), dst, sem, got, 8 + 2 * mem + k, hd) for k in range(2)]

    def scan(size, each, mates):
        dec_all(size).wait_recv()
        a_all(size, each).wait_recv()
        part = pl.ds(0, each)

        def steps(state, keep):
            for k in range(size):
                if keep:
                    out_b[k, 0:each] = state.astype(BF16)
                state = jnp.exp(dec_in[k]) * state + in_a[k, 0:each].astype(F32)
            return state

        if size == 8:
            remote(e_in.at[one], e_in.at[one], f_s, f_r, c, sib).wait_recv()
            remote(t_in, t_in, t_s, t_r, c, sib).wait_recv()
            remote(lt_in, lt_in, lt_s, lt_r, c, sib).wait_recv()
            start = jnp.exp(lt_in[...]) * e_in[0:1].astype(F32) + t_in[...].astype(F32)
            steps(start, True)
        else:
            e_out[...] = steps(jnp.zeros((each, SLICE, CHAN), F32), True).astype(BF16)

            @pl.when(grp == 0)
            def _():
                e_copy().start()

            @pl.when(grp == 1)
            def _():
                lt_out[...] = dec_in[0] + dec_in[1] + dec_in[2] + dec_in[3]
                pl.semaphore_wait(rdy_e, 2)
                for cp in to_late(lambda k: e_out.at[pl.ds(k, 1)], t_in, t_s, t_r):
                    cp.start()
                for cp in to_late(lambda k: lt_out, lt_in, lt_s, lt_r):
                    cp.start()
                remote(e_in, e_in, e_s, e_r, c, sib).wait_recv()
                steps(e_in[...].astype(F32), True)

        for to in mates:
            remote(
                out_b.at[to, part], in_b.at[pl.ds(each * mem, each)],
                b_s, b_r, c - mem + to, hd,
            ).start()
        in_b[pl.ds(each * mem, each)] = out_b[mem, 0:each]

    for_group(scan)

    @pl.when(grp == 0)
    def _():
        pl.semaphore_wait(rdy_e, 2)
        for cp in to_late(lambda k: e_out.at[pl.ds(k, 1)], e_in.at[one], f_s, f_r):
            cp.start()
        kv1_late()


    def to_core(d, carry):
        for p in range(3):
            x_copy(d, p).wait_recv()
        core_copy(d).start()
        return carry

    def attend_row(d):
        core_copy(d).wait_recv()
        attend(
            kvbuf[0, z - d].reshape(2 * TOK, HEAD_DIM), kvbuf[1, z - d].reshape(2 * TOK, HEAD_DIM),
            None, False,
        )

    def near_row(d, carry):
        attend_row(d)
        return carry

    lax.fori_loop(1, near, to_core, 0)
    core_copy_own().wait_recv()

    @pl.when(xh == 1)
    def _():
        attend(
            kvbuf[0, z, 0].reshape(TOK, HEAD_DIM), kvbuf[1, z, 0].reshape(TOK, HEAD_DIM),
            None, False,
        )

    lax.fori_loop(1, near, near_row, 0)

    def forward_far(d, carry):
        @pl.when((late == 0) | (d < 4) | (d > 4))
        def _():
            forward(d, 0)

        return carry

    lax.fori_loop(near, z + 1, forward_far, 0)

    def b_all(size, each):
        some = pl.ds(0, (size - 1) * each)
        return remote(in_b.at[some], in_b.at[some], b_s, b_r, c, sib)

    for_group(lambda size, each, mates: b_all(size, each).wait_recv())
    entering = in_b[...].reshape(STATE, CHAN)
    squares = jnp.zeros((TOK, 128), F32)
    for part in range(2):
        cols = slice(part * 256, (part + 1) * 256)
        reach = jnp.dot(cb_v[...], entering[:, cols], preferred_element_type=F32)
        gated = (pre_v[:, cols] + ecx_v[:, cols] * reach) * sz_v[:, cols]
        pre_v[:, cols] = gated
        squares = squares + gated[:, :128] * gated[:, :128] + gated[:, 128:] * gated[:, 128:]
    sq_v[0] = jnp.sum(squares.T, axis=0, keepdims=True)

    def quad_copies():
        return [
            remote(sq_v.at[0], sq_v.at[1], q_s.at[0], q_r.at[0], c, sib),
            remote(sq_v.at[0], sq_v.at[2], q_s.at[1], q_r.at[1], c, hd + flip_l),
            remote(sq_v.at[0], sq_v.at[3], q_s.at[2], q_r.at[2], c, sib + flip_l),
        ]

    for cp in quad_copies():
        cp.start()

    def far_row(d, carry):
        to_core(d, 0)

        @pl.when(d > near)
        def _():
            attend_row(d - 1)

        return carry

    lax.fori_loop(near, z + 1, far_row, 0)

    for cp in quad_copies():
        cp.wait_recv()
    group_total = sq_v[0] + sq_v[1] + sq_v[2] + sq_v[3]
    scale = lax.rsqrt(group_total * (1.0 / 2048.0) + EPSILON)
    scale_col = jnp.broadcast_to(scale, (8, TOK)).T[:, 0:1]
    ssm_v[...] = (pre_v[...] * scale_col * gain_ref[...]).astype(BF16)
    ssm_out = pltpu.make_async_copy(ssm_v, ssm_hbm, loc.at[12])
    ssm_out.start()

    @pl.when(grp > 0)
    def _():
        attend_row(z)

    result = o_v[...] / l_v[...]
    for h in range(2):
        attn_v[:, h * HEAD_DIM : (h + 1) * HEAD_DIM] = result[
            :, h * TOK : (h + 1) * TOK
        ].T.astype(BF16)
    attn_out = pltpu.make_async_copy(attn_v, attn_hbm, loc.at[13])
    attn_out.start()

    @pl.when(c < N_CTX - 1)
    def _():
        for cp in halo_copies():
            cp.wait_send()

    def group_sent(size, each, mates):
        dec_all(size).wait_send()
        a_all(size, each).wait_send()
        b_all(size, each).wait_send()

    for_group(group_sent)

    @pl.when(grp == 0)
    def _():
        e_copy().wait_send()
        remote(e_out, e_in, f_s, f_r, c, sib).wait_send()

    @pl.when(grp == 1)
    def _():
        remote(e_out, e_in, t_s, t_r, c, sib).wait_send()
        two = pl.ds(0, 2)
        remote(dec_in.at[two], dec_in.at[two], lt_s, lt_r, c, sib).wait_send()

    def kv1_sent(d, carry):
        kv1_copy(d).wait_send()
        return carry

    lax.fori_loop(1, z_last + 1 - z, kv1_sent, 0)

    @pl.when(grp == 0)
    def _():
        for row in (2, 3):
            kv1_copy(row - z).wait_send()

    @pl.when(late == 0)
    def _():
        kv1_copy(4).wait_send()

    @pl.when(late == 1)
    def _():
        for e in range(1, 4):
            relay_copy(e).wait_send()

    def row_sent(d, carry):
        for p in range(3):
            x_copy(d, p).wait_send()
        core_copy(d).wait_send()
        return carry

    lax.fori_loop(1, z + 1, row_sent, 0)
    for p in (1, 2):
        x_copy(0, p).wait_send()
    core_copy_own().wait_send()
    for cp in quad_copies():
        cp.wait_send()
    ssm_out.wait()
    attn_out.wait()


def hand_over(ssm_in, attn_in, ssm_ref, attn_ref, ssm_v, attn_v, sems):
    into = [
        pltpu.make_async_copy(ssm_in, ssm_v, sems.at[0]),
        pltpu.make_async_copy(attn_in, attn_v, sems.at[1]),
    ]
    out = [
        pltpu.make_async_copy(ssm_v, ssm_ref, sems.at[2]),
        pltpu.make_async_copy(attn_v, attn_ref, sems.at[3]),
    ]
    for cp in into:
        cp.start()
    for cp, later in zip(into, out):
        cp.wait()
        later.start()
    for cp in out:
        cp.wait()


def local(
    x_in, z_in, bc_in, dt_raw, a_log, d_skip, conv_x, conv_bc, norm_gain, queries, keys_values
):
    hbm = pl.BlockSpec(memory_space=pltpu.HBM)
    dma = pltpu.SemaphoreType.DMA
    out_shape = (
        jax.ShapeDtypeStruct((TOK, CHAN), BF16),
        jax.ShapeDtypeStruct((TOK, 2 * HEAD_DIM), BF16),
    )
    mixed = pl.pallas_call(
        kernel,
        out_shape=out_shape,
        in_specs=[hbm] * 11,
        out_specs=(hbm, hbm),
        scratch_shapes=[
            pltpu.VMEM((HEADS, TOK), F32),
            pltpu.SMEM((HEADS,), F32),
            pltpu.SMEM((HEADS,), F32),
            pltpu.VMEM((CONV, CHAN), BF16),
            pltpu.VMEM((CONV, 2 * GROUPS * STATE), BF16),
            pltpu.VMEM((1, CHAN), F32),
            pltpu.VMEM((TOK, CHAN), BF16),
            pltpu.VMEM((TOK, CHAN), BF16),
            pltpu.VMEM((TOK, STATE), BF16),
            pltpu.VMEM((TOK, STATE), BF16),
            pltpu.VMEM((TOK, 2 * HEAD_DIM), BF16),
            pltpu.VMEM((2 * TOK, HEAD_DIM), BF16),
            pltpu.VMEM((2, ROWS_Z, 2, 2, 2, QUART, HEAD_DIM), BF16),
            pltpu.VMEM((16, CHAN), BF16),
            pltpu.VMEM((2, 16, STATE), BF16),
            pltpu.VMEM((8 + TOK, CHAN), F32),
            pltpu.VMEM((8 + TOK, 2 * STATE), F32),
            pltpu.VMEM((TOK, STATE), F32),
            pltpu.VMEM((8, SLICE, CHAN), BF16),
            pltpu.VMEM((8, 2, SLICE, CHAN), BF16),
            pltpu.VMEM((8, 2, SLICE, CHAN), BF16),
            pltpu.VMEM((8, SLICE, CHAN), BF16),
            pltpu.VMEM((2, SLICE, CHAN), BF16),
            pltpu.VMEM((2, SLICE, CHAN), BF16),
            pltpu.VMEM((1, SLICE, CHAN), BF16),
            pltpu.VMEM((1, CHAN), F32),
            pltpu.VMEM((1, CHAN), F32),
            pltpu.VMEM((1, CHAN), F32),
            pltpu.VMEM((8, 1, CHAN), F32),
            pltpu.VMEM((TOK, CHAN), F32),
            pltpu.VMEM((TOK, CHAN), F32),
            pltpu.VMEM((TOK, CHAN), F32),
            pltpu.VMEM((TOK, STATE), BF16),
            pltpu.VMEM((4, 1, TOK), F32),
            pltpu.VMEM((1, 2 * TOK), F32),
            pltpu.VMEM((1, 2 * TOK), F32),
            pltpu.VMEM((HEAD_DIM, 2 * TOK), F32),
            pltpu.VMEM((TOK, CHAN), BF16),
            pltpu.VMEM((TOK, 2 * HEAD_DIM), BF16),
            dma((14,)), dma((3,)), dma((3,)),
            dma(()), dma(()), dma(()), dma(()), dma(()), dma(()), dma(()), dma(()),
            dma(()), dma(()), dma(()), dma(()), dma(()), dma(()),
            dma((3,)), dma((3,)), dma((ROWS_Z,)), dma((ROWS_Z,)),
            dma((ROWS_Z, 3)), dma((ROWS_Z, 3)), dma((ROWS_Z,)), dma((ROWS_Z,)),
            pltpu.SemaphoreType.REGULAR((2,)),
            pltpu.SemaphoreType.REGULAR, dma((4,)),
        ],
        compiler_params=pltpu.CompilerParams(
            collective_id=0, has_side_effects=True, vmem_limit_bytes=64 * 1024 * 1024
        ),
        name="mixer",
    )(
        x_in, z_in, bc_in, dt_raw, a_log, d_skip, conv_x, conv_bc,
        norm_gain.reshape(1, CHAN), queries,
        keys_values.reshape(2, 2, 2, QUART, GROUPS * HEAD_DIM),
    )
    return pl.pallas_call(
        hand_over,
        out_shape=out_shape,
        in_specs=[hbm, hbm],
        out_specs=(hbm, hbm),
        scratch_shapes=[
            pltpu.VMEM((TOK, CHAN), BF16), pltpu.VMEM((TOK, 2 * HEAD_DIM), BF16), dma((4,)),
        ],
        name="hand_over",
    )(*mixed)


def solution(mesh):
    placed = (
        P("ctx", "head"),
        P("ctx", "head"),
        P("ctx", None),
        P("head", "ctx"),
        P("head"),
        P("head"),
        P(None, "head"),
        P(),
        P("head"),
        P("ctx", "head"),
        P(None, "ctx", None),
    )
    return jax.shard_map(
        local,
        mesh=mesh,
        in_specs=placed,
        out_specs=(P("ctx", "head"), P("ctx", "head")),
        check_vma=False,
    )
```

```python
import functools
import math

import jax
import jax.numpy as jnp
from jax import lax
from jax.experimental import pallas as pl
from jax.experimental.pallas import tpu as pltpu
from jax.sharding import PartitionSpec as P

GROUPS = 8
STATE = 128
HEAD_DIM = 128
CONV = 4
TOK = 256
HEADS = 8
CHAN = 512
N_CTX = 16
BLOCK = 128
ROWS_Z = 8
SLICE = STATE // 8
QUART = TOK // 4
EPSILON = 1e-05
NEGATIVE = -1e30
HIGH = lax.Precision.HIGHEST
MESH = pl.DeviceIdType.MESH
F32 = jnp.float32
BF16 = jnp.bfloat16
PEERS = ((0, 1), (1, 0), (1, 1))
EXP_SCALE = math.log2(math.e) / math.sqrt(HEAD_DIM)


def silu(v):
    return v / (1.0 + jnp.exp(-v))


def conv_rows(pad_ref, taps, cols, rows):
    total = jnp.zeros((rows, cols.size), F32)
    for k in range(CONV):
        total = total + pad_ref[5 + k : 5 + k + rows, cols] * taps[k : k + 1]
    return silu(total)


def kernel(
    x_hbm, z_hbm, bc_hbm, dt_hbm, alog_hbm, dskip_hbm, cx_hbm, cbc_hbm, gain_hbm, q_hbm, kv_hbm,
    ssm_hbm, attn_hbm,
    dt_ref, alog_ref, dskip_ref, cx_ref, cbc_ref, gain_ref,
    x_v, z_v, b_v, c_v, q_v, q2_v, kvbuf, halo_x, halo_bc, pad_x, pad_bc, bf_v,
    st_send, in_a, out_b, in_b, e_out, e_in, t_in, lt_out, lt_in, dec_send, dec_in, pre_v, sz_v, ecx_v, cb_v, sq_v,
    m_v, l_v, o_v, ssm_v, attn_v,
    loc, h_s, h_r, d_s, d_r, a_s, a_r, b_s, b_r, e_s, e_r, f_s, f_r, t_s, t_r, lt_s, lt_r, q_s, q_r, s1_s, s1_r,
    x_s, x_r, c_s, c_r, rdy, rdy_e, r_s,
):
    c = lax.axis_index("ctx")
    hd = lax.axis_index("head")
    z, xh = lax.div(c, 2), lax.rem(c, 2)
    late = lax.div(c, 8)
    grp = lax.div(c, 4) - lax.div(c, 12)
    mem = (1 - late) * lax.rem(c, 4) + late * (c - 8)
    z_first = 2 * grp
    z_last = z_first + 1 + 2 * late
    y, qi = lax.div(hd, 4), lax.rem(hd, 4)
    xl, core = lax.div(qi, 2), lax.rem(qi, 2)
    flip_c = 1 - 2 * xh
    flip_l = 2 * (1 - 2 * xl)
    sib = hd + 1 - 2 * core
    hf = hd + flip_l
    ycol = pl.multiple_of(y * 128, 128)
    ycol2 = pl.multiple_of(GROUPS * STATE + y * 128, 128)

    def for_group(act):
        @pl.when(late == 0)
        def _():
            act(4, 2, [lax.rem(mem + e, 4) for e in range(1, 4)])

        @pl.when(late == 1)
        def _():
            act(8, 1, [lax.rem(mem + e, 8) for e in range(1, 8)])

    def remote(src, dst, ss, rs, ctx, head):
        return pltpu.make_async_remote_copy(
            src_ref=src, dst_ref=dst, send_sem=ss, recv_sem=rs,
            device_id=(ctx, head), device_id_type=MESH,
        )

    small = [
        pltpu.make_async_copy(src, dst, loc.at[i])
        for i, (src, dst) in enumerate(
            (
                (dt_hbm, dt_ref), (alog_hbm, alog_ref), (dskip_hbm, dskip_ref),
                (cx_hbm, cx_ref), (cbc_hbm, cbc_ref), (gain_hbm, gain_ref),
            )
        )
    ]
    load_x = pltpu.make_async_copy(x_hbm, x_v, loc.at[6])
    load_b = pltpu.make_async_copy(bc_hbm.at[:, pl.ds(ycol, 128)], b_v, loc.at[7])
    load_c = pltpu.make_async_copy(bc_hbm.at[:, pl.ds(ycol2, 128)], c_v, loc.at[8])
    load_q = pltpu.make_async_copy(q_hbm, q_v, loc.at[9])
    load_z = pltpu.make_async_copy(z_hbm, z_v, loc.at[10])
    load_kv = pltpu.make_async_copy(
        kv_hbm.at[:, :, :, :, pl.ds(ycol, 128)], kvbuf.at[:, z, xh], loc.at[11]
    )
    for cp in small + [load_b, load_c, load_x, load_kv, load_q, load_z]:
        cp.start()

    barrier = pltpu.get_barrier_semaphore()

    def greet(ctx, head):
        pl.semaphore_signal(barrier, inc=1, device_id=(ctx, head), device_id_type=MESH)

    def greet_mates(size, each, mates):
        for to in mates:
            greet(c - mem + to, hd)
            greet(c - mem + to, hf)

    for_group(greet_mates)
    greet(c, sib)
    greet(c, hd + flip_l)
    greet(c, sib + flip_l)
    greet(c + flip_c, hd + flip_l)

    @pl.when((mem == 0) & (c > 0))
    def _():
        greet(c - 1, hd)

    @pl.when(grp < 2)
    def _():
        for k in range(2):
            greet(8 + 2 * mem + k, hd)

    @pl.when(grp == 0)
    def _():
        for row in (2, 3):
            greet(2 * row + xh, hd)

    @pl.when(grp < 2)
    def _():
        greet(c + 8, hd)

    for cp in small:
        cp.wait()
    a_log = jnp.zeros((HEADS, 1), F32)
    head_row = lax.broadcasted_iota(jnp.int32, (HEADS, 1), 0)
    for h in range(HEADS):
        a_log = jnp.where(head_row == h, alog_ref[h], a_log)
    step = jnp.log(1.0 + jnp.exp(dt_ref[...]))
    cum = -jnp.exp(a_log) * step
    lane = lax.broadcasted_iota(jnp.int32, (HEADS, TOK), 1)
    shift = 1
    while shift < TOK:
        cum = cum + jnp.where(lane >= shift, pltpu.roll(cum, shift, 1), 0.0)
        shift *= 2
    last = cum[:, TOK - 1 : TOK]
    of_head = (
        lax.div(lax.broadcasted_iota(jnp.int32, (HEADS, CHAN), 1), CHAN // HEADS)
        == lax.broadcasted_iota(jnp.int32, (HEADS, CHAN), 0)
    )
    spread = jnp.where(of_head, 1.0, 0.0).astype(F32)
    dec_send[...] = jnp.sum(jnp.where(of_head, last, 0.0), axis=0, keepdims=True)
    tail = jnp.exp(last - cum) * step
    tail_x = jnp.dot(tail.T, spread, precision=HIGH, preferred_element_type=F32)

    greeted = 2 * (3 + 4 * late) + 4 + jnp.where(grp == 1, 2, 0) + 3 * late + jnp.where((mem == 3) & (late == 0), 1, 0)
    pl.semaphore_wait(barrier, greeted)

    def halo_copies():
        tail_rows = pl.ds(TOK - 16, 16)
        return [
            remote(x_hbm.at[tail_rows, :], halo_x, h_s.at[0], h_r.at[0], c + 1, hd),
            remote(
                bc_hbm.at[tail_rows, pl.ds(ycol, 128)], halo_bc.at[0],
                h_s.at[1], h_r.at[1], c + 1, hd,
            ),
            remote(
                bc_hbm.at[tail_rows, pl.ds(ycol2, 128)], halo_bc.at[1],
                h_s.at[2], h_r.at[2], c + 1, hd,
            ),
        ]

    @pl.when(c < N_CTX - 1)
    def _():
        for cp in halo_copies():
            cp.start()

    def say_ready(sem, ctx):
        pl.semaphore_signal(sem, inc=1, device_id=(ctx, hd), device_id_type=MESH)

    @pl.when(grp == 1)
    def _():
        for row in range(2):
            say_ready(rdy.at[0], 2 * row + xh)

    @pl.when(grp == 2)
    def _():
        say_ready(rdy.at[1], c - 8)
        say_ready(rdy_e, lax.div(mem, 2))
        say_ready(rdy_e, 4 + lax.div(mem, 2))

    def dec_copy(to):
        return remote(dec_send, dec_in.at[mem], d_s, d_r, c - mem + to, hf)

    def dec_start(size, each, mates):
        for to in mates + [mem]:
            dec_copy(to).start()

    for_group(dec_start)

    def kv1_copy(d):
        return remote(
            kvbuf.at[:, z, xh, xl, core], kvbuf.at[:, z, xh, xl, core],
            s1_s.at[d], s1_r.at[d], c + 2 * d, hd,
        )

    def kv1_got(d):
        piece = kvbuf.at[:, z - d, xh, xl, core]
        return remote(piece, piece, s1_s.at[d], s1_r.at[d], c, sib)

    def kv1_start(d, carry):
        kv1_copy(d).start()
        return carry

    def kv1_next():
        pl.semaphore_wait(rdy.at[0], 2)
        for row in (2, 3):
            kv1_copy(row - z).start()

    def kv1_late():
        pl.semaphore_wait(rdy.at[1], 1)
        kv1_copy(4).start()

    def relay_copy(e):
        row = 4 + lax.rem(z - 4 + e, 4)
        piece = kvbuf.at[:, z - 4, xh, xl, core]
        return remote(piece, piece, r_s.at[e], s1_r.at[row + 4 - z], 2 * row + xh, hd)

    def x_copy(d, p):
        fh, fl = PEERS[p]
        piece = kvbuf.at[:, z - d, xh, xl, core]
        return remote(piece, piece, x_s.at[d, p], x_r.at[d, p], c + fh * flip_c, hd + fl * flip_l)

    def core_copy(d):
        piece = kvbuf.at[:, z - d, :, :, core]
        return remote(piece, piece, c_s.at[d], c_r.at[d], c, sib)

    def core_copy_own():
        piece = kvbuf.at[:, z, 1 - xh, :, core]
        return remote(piece, piece, c_s.at[0], c_r.at[0], c, sib)

    load_kv.wait()
    for p in (1, 2):
        x_copy(0, p).start()
    lax.fori_loop(1, z_last + 1 - z, kv1_start, 0)

    taps_b = cbc_ref[:, pl.ds(ycol, 128)].astype(F32)
    taps_c = cbc_ref[:, pl.ds(ycol2, 128)].astype(F32)
    taps_x = cx_ref[...].astype(F32)
    pad_bc[0:8] = jnp.zeros((8, 2 * STATE), F32)
    pad_x[0:8] = jnp.zeros((8, CHAN), F32)
    load_b.wait()
    load_c.wait()
    pad_bc[8:, 0:STATE] = b_v[...].astype(F32)
    pad_bc[8:, STATE:] = c_v[...].astype(F32)

    def convolve(rows):
        bf_v[0:rows] = conv_rows(pad_bc, taps_b, pl.ds(0, STATE), rows)
        cb_v[0:rows] = conv_rows(pad_bc, taps_c, pl.ds(STATE, STATE), rows).astype(BF16)
        x_v[0:rows] = conv_rows(pad_x, taps_x, pl.ds(0, CHAN), rows).astype(BF16)

    load_x.wait()
    pad_x[8:] = x_v[...].astype(F32)
    convolve(TOK)

    def attend(keys, values, mask, first):
        logits = lax.dot_general(
            keys, q2_v[...], (((1,), (1,)), ((), ())), preferred_element_type=F32
        )
        if mask is not None:
            logits = jnp.where(mask, logits, NEGATIVE)
        top = jnp.max(logits, axis=0, keepdims=True)
        if not first:
            top = jnp.maximum(m_v[...], top)
        grown = jnp.exp2((logits - top) * EXP_SCALE)
        if mask is not None:
            grown = jnp.where(mask, grown, 0.0)
        den = jnp.sum(grown, axis=0, keepdims=True)
        got = jnp.dot(values.T, grown.astype(BF16), preferred_element_type=F32)
        if first:
            l_v[...] = den
            o_v[...] = got
        else:
            shrink = jnp.exp2((m_v[...] - top) * EXP_SCALE)
            l_v[...] = l_v[...] * shrink + den
            o_v[...] = o_v[...] * shrink + got
        m_v[...] = top

    load_q.wait()
    q2_v[0:TOK] = q_v[:, :HEAD_DIM]
    q2_v[TOK:] = q_v[:, HEAD_DIM:]
    key_at = lax.broadcasted_iota(jnp.int32, (TOK, 2 * TOK), 0)
    query_at = lax.rem(lax.broadcasted_iota(jnp.int32, (TOK, 2 * TOK), 1), TOK)
    attend(
        kvbuf[0, z, xh].reshape(TOK, HEAD_DIM), kvbuf[1, z, xh].reshape(TOK, HEAD_DIM),
        key_at <= query_at, True,
    )
    @pl.when(c > 0)
    def _():
        for cp in halo_copies():
            cp.wait_recv()
        pad_bc[0:8, 0:STATE] = halo_bc[0].astype(F32)[8:16]
        pad_bc[0:8, STATE:] = halo_bc[1].astype(F32)[8:16]
        pad_x[0:8] = halo_x[...].astype(F32)[8:16]
        convolve(16)

    b_t = bf_v[...].T.astype(BF16)
    carried = (tail_x * x_v[...].astype(F32)).astype(BF16)
    state = jnp.dot(b_t, carried, preferred_element_type=F32).astype(BF16)
    st_send[...] = state.reshape(8, SLICE, CHAN)

    def a_start(size, each, mates):
        for to in mates + [mem]:
            remote(
                st_send.at[pl.ds(each * to, each)], in_a.at[mem, pl.ds(0, each)],
                a_s, a_r, c - mem + to, hf,
            ).start()

    def a_all():
        return remote(st_send, st_send, a_s, a_r, c, sib)

    for_group(a_start)

    @pl.when(grp == 0)
    def _():
        kv1_next()


    scores = jnp.dot(cb_v[...], b_t, preferred_element_type=F32)
    t_at = lax.broadcasted_iota(jnp.int32, (TOK, TOK), 0)
    s_at = lax.broadcasted_iota(jnp.int32, (TOK, TOK), 1)
    scores = jnp.where(s_at <= t_at, scores, 0.0)
    cum_t = cum.T
    skip_row = jnp.zeros((1, CHAN), F32)
    head_of_lane = lax.div(lax.broadcasted_iota(jnp.int32, (1, CHAN), 1), CHAN // HEADS)
    for h in range(HEADS):
        skip_row = jnp.where(head_of_lane == h, dskip_ref[h], skip_row)
    left = lax.broadcasted_iota(jnp.int32, (BLOCK, 128), 1) < 64
    for low in (0, BLOCK):
        rows, upto = slice(low, low + BLOCK), low + BLOCK
        for pair in range(HEADS // 2):
            cols = slice(128 * pair, 128 * pair + 128)
            both = []
            for h in (2 * pair, 2 * pair + 1):
                gap = jnp.minimum(cum_t[rows, h : h + 1] - cum[h : h + 1, :upto], 0.0)
                weights = (scores[rows, :upto] * jnp.exp(gap) * step[h : h + 1, :upto]).astype(BF16)
                both.append(jnp.dot(weights, x_v[:upto, cols], preferred_element_type=F32))
            pre_v[rows, cols] = (
                jnp.where(left, both[0], both[1])
                + skip_row[:, cols] * x_v[rows, cols].astype(F32)
            )
    ecx_v[...] = jnp.dot(jnp.exp(cum).T, spread, precision=HIGH, preferred_element_type=F32)
    load_z.wait()
    sz_v[...] = silu(z_v[...].astype(F32))

    @pl.when(grp == 1)
    def _():
        kv1_late()

    for p in (1, 2):
        x_copy(0, p).wait_recv()
    core_copy_own().start()

    def forward(d, carry):
        kv1_got(d).wait_recv()
        for p in (1, 0, 2):
            x_copy(d, p).start()
        return carry

    near = z - z_first + 1
    lax.fori_loop(1, near, forward, 0)

    @pl.when(late == 1)
    def _():
        kv1_got(4).wait_recv()
        for e in range(1, 4):
            relay_copy(e).start()
        for p in range(3):
            x_copy(4, p).start()

    def dec_all(size):
        some = pl.ds(0, size)
        return remote(dec_in.at[some], dec_in.at[some], d_s, d_r, c, sib)

    one = pl.ds(0, 1)

    def e_copy():
        return remote(e_out, e_in, e_s, e_r, c + 4, hd)

    def to_late(src, dst, sem, got):
        return [remote(src(k), dst, sem, got, 8 + 2 * mem + k, hd) for k in range(2)]

    def scan(size, each, mates):
        dec_all(size).wait_recv()
        a_all().wait_recv()
        part = pl.ds(0, each)

        def steps(state, keep):
            for k in range(size):
                if keep:
                    out_b[k, 0:each] = state.astype(BF16)
                state = jnp.exp(dec_in[k]) * state + in_a[k, 0:each].astype(F32)
            return state

        if size == 8:
            remote(e_in.at[one], e_in.at[one], f_s, f_r, c, sib).wait_recv()
            remote(t_in, t_in, t_s, t_r, c, sib).wait_recv()
            remote(lt_in, lt_in, lt_s, lt_r, c, sib).wait_recv()
            start = jnp.exp(lt_in[...]) * e_in[0:1].astype(F32) + t_in[...].astype(F32)
            steps(start, True)
        else:
            e_out[...] = steps(jnp.zeros((each, SLICE, CHAN), F32), True).astype(BF16)

            @pl.when(grp == 0)
            def _():
                e_copy().start()
                kv1_late()

            @pl.when(grp == 1)
            def _():
                lt_out[...] = dec_in[0] + dec_in[1] + dec_in[2] + dec_in[3]
                pl.semaphore_wait(rdy_e, 2)
                for cp in to_late(lambda k: e_out.at[pl.ds(k, 1)], t_in, t_s, t_r):
                    cp.start()
                for cp in to_late(lambda k: lt_out, lt_in, lt_s, lt_r):
                    cp.start()
                remote(e_in, e_in, e_s, e_r, c, sib).wait_recv()
                steps(e_in[...].astype(F32), True)

        for to in mates + [mem]:
            remote(
                out_b.at[to, part], in_b.at[pl.ds(each * mem, each)],
                b_s, b_r, c - mem + to, hf,
            ).start()

    for_group(scan)

    @pl.when(grp == 0)
    def _():
        pl.semaphore_wait(rdy_e, 2)
        for cp in to_late(lambda k: e_out.at[pl.ds(k, 1)], e_in.at[one], f_s, f_r):
            cp.start()


    def to_core(d, carry):
        for p in range(3):
            x_copy(d, p).wait_recv()
        core_copy(d).start()
        return carry

    def attend_row(d):
        core_copy(d).wait_recv()
        attend(
            kvbuf[0, z - d].reshape(2 * TOK, HEAD_DIM), kvbuf[1, z - d].reshape(2 * TOK, HEAD_DIM),
            None, False,
        )

    def near_row(d, carry):
        attend_row(d)
        return carry

    def forward_far(d, carry):
        @pl.when((late == 0) | (d < 4) | (d > 4))
        def _():
            forward(d, 0)

        return carry

    lax.fori_loop(near, z + 1, forward_far, 0)
    lax.fori_loop(1, near, to_core, 0)
    core_copy_own().wait_recv()

    @pl.when(xh == 1)
    def _():
        attend(
            kvbuf[0, z, 0].reshape(TOK, HEAD_DIM), kvbuf[1, z, 0].reshape(TOK, HEAD_DIM),
            None, False,
        )

    lax.fori_loop(1, near, near_row, 0)


    def b_all():
        return remote(in_b, in_b, b_s, b_r, c, sib)

    b_all().wait_recv()
    entering = in_b[...].reshape(STATE, CHAN)
    squares = jnp.zeros((TOK, 128), F32)
    for part in range(2):
        cols = slice(part * 256, (part + 1) * 256)
        reach = jnp.dot(cb_v[...], entering[:, cols], preferred_element_type=F32)
        gated = (pre_v[:, cols] + ecx_v[:, cols] * reach) * sz_v[:, cols]
        pre_v[:, cols] = gated
        squares = squares + gated[:, :128] * gated[:, :128] + gated[:, 128:] * gated[:, 128:]
    sq_v[0] = jnp.sum(squares.T, axis=0, keepdims=True)

    def quad_copies():
        return [
            remote(sq_v.at[0], sq_v.at[1], q_s.at[0], q_r.at[0], c, sib),
            remote(sq_v.at[0], sq_v.at[2], q_s.at[1], q_r.at[1], c, hd + flip_l),
            remote(sq_v.at[0], sq_v.at[3], q_s.at[2], q_r.at[2], c, sib + flip_l),
        ]

    for cp in quad_copies():
        cp.start()

    def far_row(d, carry):
        to_core(d, 0)

        @pl.when(d > near)
        def _():
            attend_row(d - 1)

        return carry

    lax.fori_loop(near, z + 1, far_row, 0)

    for cp in quad_copies():
        cp.wait_recv()
    group_total = sq_v[0] + sq_v[1] + sq_v[2] + sq_v[3]
    scale = lax.rsqrt(group_total * (1.0 / 2048.0) + EPSILON)
    scale_col = jnp.broadcast_to(scale, (8, TOK)).T[:, 0:1]
    ssm_v[...] = (pre_v[...] * scale_col * gain_ref[...]).astype(BF16)
    ssm_out = pltpu.make_async_copy(ssm_v, ssm_hbm, loc.at[12])
    ssm_out.start()

    @pl.when(grp > 0)
    def _():
        attend_row(z)

    result = o_v[...] / l_v[...]
    for h in range(2):
        attn_v[:, h * HEAD_DIM : (h + 1) * HEAD_DIM] = result[
            :, h * TOK : (h + 1) * TOK
        ].T.astype(BF16)
    attn_out = pltpu.make_async_copy(attn_v, attn_hbm, loc.at[13])
    attn_out.start()

    @pl.when(c < N_CTX - 1)
    def _():
        for cp in halo_copies():
            cp.wait_send()

    def group_sent(size, each, mates):
        dec_all(size).wait_send()
        a_all().wait_send()
        b_all().wait_send()

    for_group(group_sent)

    @pl.when(grp == 0)
    def _():
        e_copy().wait_send()
        remote(e_out, e_in, f_s, f_r, c, sib).wait_send()

    @pl.when(grp == 1)
    def _():
        remote(e_out, e_in, t_s, t_r, c, sib).wait_send()
        two = pl.ds(0, 2)
        remote(dec_in.at[two], dec_in.at[two], lt_s, lt_r, c, sib).wait_send()

    def kv1_sent(d, carry):
        kv1_copy(d).wait_send()
        return carry

    lax.fori_loop(1, z_last + 1 - z, kv1_sent, 0)

    @pl.when(grp == 0)
    def _():
        for row in (2, 3):
            kv1_copy(row - z).wait_send()

    @pl.when(late == 0)
    def _():
        kv1_copy(4).wait_send()

    @pl.when(late == 1)
    def _():
        for e in range(1, 4):
            relay_copy(e).wait_send()

    def row_sent(d, carry):
        for p in range(3):
            x_copy(d, p).wait_send()
        core_copy(d).wait_send()
        return carry

    lax.fori_loop(1, z + 1, row_sent, 0)
    for p in (1, 2):
        x_copy(0, p).wait_send()
    core_copy_own().wait_send()
    for cp in quad_copies():
        cp.wait_send()
    ssm_out.wait()
    attn_out.wait()


def hand_over(ssm_in, attn_in, ssm_ref, attn_ref, ssm_v, attn_v, sems):
    into = [
        pltpu.make_async_copy(ssm_in, ssm_v, sems.at[0]),
        pltpu.make_async_copy(attn_in, attn_v, sems.at[1]),
    ]
    out = [
        pltpu.make_async_copy(ssm_v, ssm_ref, sems.at[2]),
        pltpu.make_async_copy(attn_v, attn_ref, sems.at[3]),
    ]
    for cp in into:
        cp.start()
    for cp, later in zip(into, out):
        cp.wait()
        later.start()
    for cp in out:
        cp.wait()


def local(
    x_in, z_in, bc_in, dt_raw, a_log, d_skip, conv_x, conv_bc, norm_gain, queries, keys_values
):
    hbm = pl.BlockSpec(memory_space=pltpu.HBM)
    dma = pltpu.SemaphoreType.DMA
    out_shape = (
        jax.ShapeDtypeStruct((TOK, CHAN), BF16),
        jax.ShapeDtypeStruct((TOK, 2 * HEAD_DIM), BF16),
    )
    mixed = pl.pallas_call(
        kernel,
        out_shape=out_shape,
        in_specs=[hbm] * 11,
        out_specs=(hbm, hbm),
        scratch_shapes=[
            pltpu.VMEM((HEADS, TOK), F32),
            pltpu.SMEM((HEADS,), F32),
            pltpu.SMEM((HEADS,), F32),
            pltpu.VMEM((CONV, CHAN), BF16),
            pltpu.VMEM((CONV, 2 * GROUPS * STATE), BF16),
            pltpu.VMEM((1, CHAN), F32),
            pltpu.VMEM((TOK, CHAN), BF16),
            pltpu.VMEM((TOK, CHAN), BF16),
            pltpu.VMEM((TOK, STATE), BF16),
            pltpu.VMEM((TOK, STATE), BF16),
            pltpu.VMEM((TOK, 2 * HEAD_DIM), BF16),
            pltpu.VMEM((2 * TOK, HEAD_DIM), BF16),
            pltpu.VMEM((2, ROWS_Z, 2, 2, 2, QUART, HEAD_DIM), BF16),
            pltpu.VMEM((16, CHAN), BF16),
            pltpu.VMEM((2, 16, STATE), BF16),
            pltpu.VMEM((8 + TOK, CHAN), F32),
            pltpu.VMEM((8 + TOK, 2 * STATE), F32),
            pltpu.VMEM((TOK, STATE), F32),
            pltpu.VMEM((8, SLICE, CHAN), BF16),
            pltpu.VMEM((8, 2, SLICE, CHAN), BF16),
            pltpu.VMEM((8, 2, SLICE, CHAN), BF16),
            pltpu.VMEM((8, SLICE, CHAN), BF16),
            pltpu.VMEM((2, SLICE, CHAN), BF16),
            pltpu.VMEM((2, SLICE, CHAN), BF16),
            pltpu.VMEM((1, SLICE, CHAN), BF16),
            pltpu.VMEM((1, CHAN), F32),
            pltpu.VMEM((1, CHAN), F32),
            pltpu.VMEM((1, CHAN), F32),
            pltpu.VMEM((8, 1, CHAN), F32),
            pltpu.VMEM((TOK, CHAN), F32),
            pltpu.VMEM((TOK, CHAN), F32),
            pltpu.VMEM((TOK, CHAN), F32),
            pltpu.VMEM((TOK, STATE), BF16),
            pltpu.VMEM((4, 1, TOK), F32),
            pltpu.VMEM((1, 2 * TOK), F32),
            pltpu.VMEM((1, 2 * TOK), F32),
            pltpu.VMEM((HEAD_DIM, 2 * TOK), F32),
            pltpu.VMEM((TOK, CHAN), BF16),
            pltpu.VMEM((TOK, 2 * HEAD_DIM), BF16),
            dma((14,)), dma((3,)), dma((3,)),
            dma(()), dma(()), dma(()), dma(()), dma(()), dma(()), dma(()), dma(()),
            dma(()), dma(()), dma(()), dma(()), dma(()), dma(()),
            dma((3,)), dma((3,)), dma((ROWS_Z,)), dma((ROWS_Z,)),
            dma((ROWS_Z, 3)), dma((ROWS_Z, 3)), dma((ROWS_Z,)), dma((ROWS_Z,)),
            pltpu.SemaphoreType.REGULAR((2,)),
            pltpu.SemaphoreType.REGULAR, dma((4,)),
        ],
        compiler_params=pltpu.CompilerParams(
            collective_id=0, has_side_effects=True, vmem_limit_bytes=64 * 1024 * 1024
        ),
        name="mixer",
    )(
        x_in, z_in, bc_in, dt_raw, a_log, d_skip, conv_x, conv_bc,
        norm_gain.reshape(1, CHAN), queries,
        keys_values.reshape(2, 2, 2, QUART, GROUPS * HEAD_DIM),
    )
    return pl.pallas_call(
        hand_over,
        out_shape=out_shape,
        in_specs=[hbm, hbm],
        out_specs=(hbm, hbm),
        scratch_shapes=[
            pltpu.VMEM((TOK, CHAN), BF16), pltpu.VMEM((TOK, 2 * HEAD_DIM), BF16), dma((4,)),
        ],
        name="hand_over",
    )(*mixed)


def solution(mesh):
    placed = (
        P("ctx", "head"),
        P("ctx", "head"),
        P("ctx", None),
        P("head", "ctx"),
        P("head"),
        P("head"),
        P(None, "head"),
        P(),
        P("head"),
        P("ctx", "head"),
        P(None, "ctx", None),
    )
    return jax.shard_map(
        local,
        mesh=mesh,
        in_specs=placed,
        out_specs=(P("ctx", "head"), P("ctx", "head")),
        check_vma=False,
    )
```

```python
import functools
import math

import jax
import jax.numpy as jnp
from jax import lax
from jax.experimental import pallas as pl
from jax.experimental.pallas import tpu as pltpu
from jax.sharding import PartitionSpec as P

GROUPS = 8
STATE = 128
HEAD_DIM = 128
CONV = 4
TOK = 256
HEADS = 8
CHAN = 512
N_CTX = 16
BLOCK = 128
ROWS_Z = 8
SLICE = STATE // 8
QUART = TOK // 4
EPSILON = 1e-05
NEGATIVE = -1e30
HIGH = lax.Precision.HIGHEST
MESH = pl.DeviceIdType.MESH
F32 = jnp.float32
BF16 = jnp.bfloat16
PEERS = ((0, 1), (1, 0), (1, 1))
EXP_SCALE = math.log2(math.e) / math.sqrt(HEAD_DIM)


def silu(v):
    return v / (1.0 + jnp.exp(-v))


def conv_rows(pad_ref, taps, cols, rows):
    total = jnp.zeros((rows, cols.size), F32)
    for k in range(CONV):
        total = total + pad_ref[5 + k : 5 + k + rows, cols] * taps[k : k + 1]
    return silu(total)


def kernel(
    x_hbm, z_hbm, bc_hbm, dt_hbm, alog_hbm, dskip_hbm, cx_hbm, cbc_hbm, gain_hbm, q_hbm, kv_hbm,
    ssm_hbm, attn_hbm,
    dt_ref, alog_ref, dskip_ref, cx_ref, cbc_ref, gain_ref,
    x_v, z_v, b_v, c_v, q_v, q2_v, kvbuf, halo_x, halo_bc, pad_x, pad_bc, bf_v,
    st_send, in_a, out_b, in_b, e_out, e_in, t_in, lt_out, lt_in, dec_send, dec_in, pre_v, sz_v, ecx_v, cb_v, sq_v,
    m_v, l_v, o_v, ssm_v, attn_v,
    loc, h_s, h_r, d_s, d_r, a_s, a_r, b_s, b_r, e_s, e_r, f_s, f_r, t_s, t_r, lt_s, lt_r, q_s, q_r, s1_s, s1_r,
    x_s, x_r, c_s, c_r, rdy, rdy_e, r_s,
):
    c = lax.axis_index("ctx")
    hd = lax.axis_index("head")
    z, xh = lax.div(c, 2), lax.rem(c, 2)
    late = lax.div(c, 8)
    grp = lax.div(c, 4) - lax.div(c, 12)
    mem = (1 - late) * lax.rem(c, 4) + late * (c - 8)
    z_first = 2 * grp
    z_last = z_first + 1 + 2 * late
    y, qi = lax.div(hd, 4), lax.rem(hd, 4)
    xl, core = lax.div(qi, 2), lax.rem(qi, 2)
    flip_c = 1 - 2 * xh
    flip_l = 2 * (1 - 2 * xl)
    sib = hd + 1 - 2 * core
    hf = hd + flip_l
    ycol = pl.multiple_of(y * 128, 128)
    ycol2 = pl.multiple_of(GROUPS * STATE + y * 128, 128)

    def for_group(act):
        @pl.when(late == 0)
        def _():
            act(4, 2, [lax.rem(mem + e, 4) for e in range(1, 4)])

        @pl.when(late == 1)
        def _():
            act(8, 1, [lax.rem(mem + e, 8) for e in range(1, 8)])

    def remote(src, dst, ss, rs, ctx, head):
        return pltpu.make_async_remote_copy(
            src_ref=src, dst_ref=dst, send_sem=ss, recv_sem=rs,
            device_id=(ctx, head), device_id_type=MESH,
        )

    small = [
        pltpu.make_async_copy(src, dst, loc.at[i])
        for i, (src, dst) in enumerate(
            (
                (dt_hbm, dt_ref), (alog_hbm, alog_ref), (dskip_hbm, dskip_ref),
                (cx_hbm, cx_ref), (cbc_hbm, cbc_ref), (gain_hbm, gain_ref),
            )
        )
    ]
    load_x = pltpu.make_async_copy(x_hbm, x_v, loc.at[6])
    load_b = pltpu.make_async_copy(bc_hbm.at[:, pl.ds(ycol, 128)], b_v, loc.at[7])
    load_c = pltpu.make_async_copy(bc_hbm.at[:, pl.ds(ycol2, 128)], c_v, loc.at[8])
    load_q = pltpu.make_async_copy(q_hbm, q_v, loc.at[9])
    load_z = pltpu.make_async_copy(z_hbm, z_v, loc.at[10])
    load_kv = pltpu.make_async_copy(
        kv_hbm.at[:, :, :, :, pl.ds(ycol, 128)], kvbuf.at[:, z, xh], loc.at[11]
    )
    for cp in small + [load_b, load_c, load_x, load_kv, load_q, load_z]:
        cp.start()

    barrier = pltpu.get_barrier_semaphore()

    def greet(ctx, head):
        pl.semaphore_signal(barrier, inc=1, device_id=(ctx, head), device_id_type=MESH)

    def greet_mates(size, each, mates):
        for to in mates:
            greet(c - mem + to, hd)
            greet(c - mem + to, hf)

    for_group(greet_mates)
    greet(c, sib)
    greet(c, hd + flip_l)
    greet(c, sib + flip_l)
    greet(c + flip_c, hd + flip_l)

    @pl.when((mem == 0) & (c > 0))
    def _():
        greet(c - 1, hd)

    @pl.when(grp < 2)
    def _():
        for k in range(2):
            greet(8 + 2 * mem + k, hd)

    @pl.when(grp == 0)
    def _():
        for row in (2, 3):
            greet(2 * row + xh, hd)

    @pl.when(grp < 2)
    def _():
        greet(c + 8, hd)

    for cp in small:
        cp.wait()
    a_log = jnp.zeros((HEADS, 1), F32)
    head_row = lax.broadcasted_iota(jnp.int32, (HEADS, 1), 0)
    for h in range(HEADS):
        a_log = jnp.where(head_row == h, alog_ref[h], a_log)
    step = jnp.log(1.0 + jnp.exp(dt_ref[...]))
    cum = -jnp.exp(a_log) * step
    lane = lax.broadcasted_iota(jnp.int32, (HEADS, TOK), 1)
    shift = 1
    while shift < TOK:
        cum = cum + jnp.where(lane >= shift, pltpu.roll(cum, shift, 1), 0.0)
        shift *= 2
    last = cum[:, TOK - 1 : TOK]
    of_head = (
        lax.div(lax.broadcasted_iota(jnp.int32, (HEADS, CHAN), 1), CHAN // HEADS)
        == lax.broadcasted_iota(jnp.int32, (HEADS, CHAN), 0)
    )
    spread = jnp.where(of_head, 1.0, 0.0).astype(F32)
    dec_send[...] = jnp.sum(jnp.where(of_head, last, 0.0), axis=0, keepdims=True)
    tail = jnp.exp(last - cum) * step
    tail_x = jnp.dot(tail.T, spread, precision=HIGH, preferred_element_type=F32)

    greeted = 2 * (3 + 4 * late) + 4 + jnp.where(grp == 1, 2, 0) + 3 * late + jnp.where((mem == 3) & (late == 0), 1, 0)
    pl.semaphore_wait(barrier, greeted)

    def halo_copies():
        tail_rows = pl.ds(TOK - 16, 16)
        return [
            remote(x_hbm.at[tail_rows, :], halo_x, h_s.at[0], h_r.at[0], c + 1, hd),
            remote(
                bc_hbm.at[tail_rows, pl.ds(ycol, 128)], halo_bc.at[0],
                h_s.at[1], h_r.at[1], c + 1, hd,
            ),
            remote(
                bc_hbm.at[tail_rows, pl.ds(ycol2, 128)], halo_bc.at[1],
                h_s.at[2], h_r.at[2], c + 1, hd,
            ),
        ]

    @pl.when(c < N_CTX - 1)
    def _():
        for cp in halo_copies():
            cp.start()

    def say_ready(sem, ctx):
        pl.semaphore_signal(sem, inc=1, device_id=(ctx, hd), device_id_type=MESH)

    @pl.when(grp == 1)
    def _():
        for row in range(2):
            say_ready(rdy.at[0], 2 * row + xh)

    @pl.when(grp == 2)
    def _():
        say_ready(rdy.at[1], c - 8)
        say_ready(rdy_e, lax.div(mem, 2))
        say_ready(rdy_e, 4 + lax.div(mem, 2))

    def dec_copy(to):
        return remote(dec_send, dec_in.at[mem], d_s, d_r, c - mem + to, hf)

    def dec_start(size, each, mates):
        for to in mates + [mem]:
            dec_copy(to).start()

    for_group(dec_start)

    def kv1_copy(d):
        return remote(
            kvbuf.at[:, z, xh, xl, core], kvbuf.at[:, z, xh, xl, core],
            s1_s.at[d], s1_r.at[d], c + 2 * d, hd,
        )

    def kv1_got(d):
        piece = kvbuf.at[:, z - d, xh, xl, core]
        return remote(piece, piece, s1_s.at[d], s1_r.at[d], c, sib)

    def kv1_start(d, carry):
        kv1_copy(d).start()
        return carry

    def kv1_next():
        pl.semaphore_wait(rdy.at[0], 2)
        for row in (2, 3):
            kv1_copy(row - z).start()

    def kv1_late():
        pl.semaphore_wait(rdy.at[1], 1)
        kv1_copy(4).start()

    def relay_copy(e):
        row = 4 + lax.rem(z - 4 + e, 4)
        piece = kvbuf.at[:, z - 4, xh, xl, core]
        return remote(piece, piece, r_s.at[e], s1_r.at[row + 4 - z], 2 * row + xh, hd)

    def x_copy(d, p):
        fh, fl = PEERS[p]
        piece = kvbuf.at[:, z - d, xh, xl, core]
        return remote(piece, piece, x_s.at[d, p], x_r.at[d, p], c + fh * flip_c, hd + fl * flip_l)

    def core_copy(d):
        piece = kvbuf.at[:, z - d, :, :, core]
        return remote(piece, piece, c_s.at[d], c_r.at[d], c, sib)

    def core_copy_own():
        piece = kvbuf.at[:, z, 1 - xh, :, core]
        return remote(piece, piece, c_s.at[0], c_r.at[0], c, sib)

    load_kv.wait()
    for p in (1, 2):
        x_copy(0, p).start()
    lax.fori_loop(1, z_last + 1 - z, kv1_start, 0)

    taps_b = cbc_ref[:, pl.ds(ycol, 128)].astype(F32)
    taps_c = cbc_ref[:, pl.ds(ycol2, 128)].astype(F32)
    taps_x = cx_ref[...].astype(F32)
    pad_bc[0:8] = jnp.zeros((8, 2 * STATE), F32)
    pad_x[0:8] = jnp.zeros((8, CHAN), F32)
    load_b.wait()
    load_c.wait()
    pad_bc[8:, 0:STATE] = b_v[...].astype(F32)
    pad_bc[8:, STATE:] = c_v[...].astype(F32)

    def convolve(rows):
        bf_v[0:rows] = conv_rows(pad_bc, taps_b, pl.ds(0, STATE), rows)
        cb_v[0:rows] = conv_rows(pad_bc, taps_c, pl.ds(STATE, STATE), rows).astype(BF16)
        x_v[0:rows] = conv_rows(pad_x, taps_x, pl.ds(0, CHAN), rows).astype(BF16)

    load_x.wait()
    pad_x[8:] = x_v[...].astype(F32)
    convolve(TOK)

    def attend(keys, values, mask, first):
        logits = lax.dot_general(
            keys, q2_v[...], (((1,), (1,)), ((), ())), preferred_element_type=F32
        )
        if mask is not None:
            logits = jnp.where(mask, logits, NEGATIVE)
        top = jnp.max(logits, axis=0, keepdims=True)
        if not first:
            top = jnp.maximum(m_v[...], top)
        grown = jnp.exp2((logits - top) * EXP_SCALE)
        if mask is not None:
            grown = jnp.where(mask, grown, 0.0)
        den = jnp.sum(grown, axis=0, keepdims=True)
        got = jnp.dot(values.T, grown.astype(BF16), preferred_element_type=F32)
        if first:
            l_v[...] = den
            o_v[...] = got
        else:
            shrink = jnp.exp2((m_v[...] - top) * EXP_SCALE)
            l_v[...] = l_v[...] * shrink + den
            o_v[...] = o_v[...] * shrink + got
        m_v[...] = top

    load_q.wait()
    q2_v[0:TOK] = q_v[:, :HEAD_DIM]
    q2_v[TOK:] = q_v[:, HEAD_DIM:]
    key_at = lax.broadcasted_iota(jnp.int32, (TOK, 2 * TOK), 0)
    query_at = lax.rem(lax.broadcasted_iota(jnp.int32, (TOK, 2 * TOK), 1), TOK)
    attend(
        kvbuf[0, z, xh].reshape(TOK, HEAD_DIM), kvbuf[1, z, xh].reshape(TOK, HEAD_DIM),
        key_at <= query_at, True,
    )
    ecx_v[...] = jnp.dot(jnp.exp(cum).T, spread, precision=HIGH, preferred_element_type=F32)
    load_z.wait()
    sz_v[...] = silu(z_v[...].astype(F32))

    @pl.when(c > 0)
    def _():
        for cp in halo_copies():
            cp.wait_recv()
        pad_bc[0:8, 0:STATE] = halo_bc[0].astype(F32)[8:16]
        pad_bc[0:8, STATE:] = halo_bc[1].astype(F32)[8:16]
        pad_x[0:8] = halo_x[...].astype(F32)[8:16]
        convolve(16)

    b_t = bf_v[...].T.astype(BF16)
    carried = (tail_x * x_v[...].astype(F32)).astype(BF16)
    state = jnp.dot(b_t, carried, preferred_element_type=F32).astype(BF16)
    st_send[...] = state.reshape(8, SLICE, CHAN)

    def a_start(size, each, mates):
        for to in mates + [mem]:
            remote(
                st_send.at[pl.ds(each * to, each)], in_a.at[mem, pl.ds(0, each)],
                a_s, a_r, c - mem + to, hf,
            ).start()

    def a_all():
        return remote(st_send, st_send, a_s, a_r, c, sib)

    for_group(a_start)

    @pl.when(grp == 0)
    def _():
        kv1_next()


    scores = jnp.dot(cb_v[...], b_t, preferred_element_type=F32)
    t_at = lax.broadcasted_iota(jnp.int32, (TOK, TOK), 0)
    s_at = lax.broadcasted_iota(jnp.int32, (TOK, TOK), 1)
    scores = jnp.where(s_at <= t_at, scores, 0.0)
    cum_t = cum.T
    skip_row = jnp.zeros((1, CHAN), F32)
    head_of_lane = lax.div(lax.broadcasted_iota(jnp.int32, (1, CHAN), 1), CHAN // HEADS)
    for h in range(HEADS):
        skip_row = jnp.where(head_of_lane == h, dskip_ref[h], skip_row)
    left = lax.broadcasted_iota(jnp.int32, (BLOCK, 128), 1) < 64
    for low in (0, BLOCK):
        rows, upto = slice(low, low + BLOCK), low + BLOCK
        for pair in range(HEADS // 2):
            cols = slice(128 * pair, 128 * pair + 128)
            both = []
            for h in (2 * pair, 2 * pair + 1):
                gap = jnp.minimum(cum_t[rows, h : h + 1] - cum[h : h + 1, :upto], 0.0)
                weights = (scores[rows, :upto] * jnp.exp(gap) * step[h : h + 1, :upto]).astype(BF16)
                both.append(jnp.dot(weights, x_v[:upto, cols], preferred_element_type=F32))
            pre_v[rows, cols] = (
                jnp.where(left, both[0], both[1])
                + skip_row[:, cols] * x_v[rows, cols].astype(F32)
            )

    @pl.when(grp == 1)
    def _():
        kv1_late()

    for p in (1, 2):
        x_copy(0, p).wait_recv()
    core_copy_own().start()

    def forward(d, carry):
        kv1_got(d).wait_recv()
        for p in (1, 0, 2):
            x_copy(d, p).start()
        return carry

    near = z - z_first + 1
    lax.fori_loop(1, near, forward, 0)

    @pl.when(late == 1)
    def _():
        kv1_got(4).wait_recv()
        for e in range(1, 4):
            relay_copy(e).start()
        for p in range(3):
            x_copy(4, p).start()

    def dec_all(size):
        some = pl.ds(0, size)
        return remote(dec_in.at[some], dec_in.at[some], d_s, d_r, c, sib)

    one = pl.ds(0, 1)

    def e_copy():
        return remote(e_out, e_in, e_s, e_r, c + 4, hd)

    def to_late(src, dst, sem, got):
        return [remote(src(k), dst, sem, got, 8 + 2 * mem + k, hd) for k in range(2)]

    def scan(size, each, mates):
        dec_all(size).wait_recv()
        a_all().wait_recv()
        part = pl.ds(0, each)

        def steps(state, keep):
            for k in range(size):
                if keep:
                    out_b[k, 0:each] = state.astype(BF16)
                state = jnp.exp(dec_in[k]) * state + in_a[k, 0:each].astype(F32)
            return state

        if size == 8:
            remote(e_in.at[one], e_in.at[one], f_s, f_r, c, sib).wait_recv()
            remote(t_in, t_in, t_s, t_r, c, sib).wait_recv()
            remote(lt_in, lt_in, lt_s, lt_r, c, sib).wait_recv()
            start = jnp.exp(lt_in[...]) * e_in[0:1].astype(F32) + t_in[...].astype(F32)
            steps(start, True)
        else:
            e_out[...] = steps(jnp.zeros((each, SLICE, CHAN), F32), True).astype(BF16)

            @pl.when(grp == 0)
            def _():
                e_copy().start()
                kv1_late()

            @pl.when(grp == 1)
            def _():
                lt_out[...] = dec_in[0] + dec_in[1] + dec_in[2] + dec_in[3]
                pl.semaphore_wait(rdy_e, 2)
                for cp in to_late(lambda k: e_out.at[pl.ds(k, 1)], t_in, t_s, t_r):
                    cp.start()
                for cp in to_late(lambda k: lt_out, lt_in, lt_s, lt_r):
                    cp.start()
                remote(e_in, e_in, e_s, e_r, c, sib).wait_recv()
                steps(e_in[...].astype(F32), True)

        for to in mates + [mem]:
            remote(
                out_b.at[to, part], in_b.at[pl.ds(each * mem, each)],
                b_s, b_r, c - mem + to, hf,
            ).start()

    for_group(scan)

    @pl.when(grp == 0)
    def _():
        pl.semaphore_wait(rdy_e, 2)
        for cp in to_late(lambda k: e_out.at[pl.ds(k, 1)], e_in.at[one], f_s, f_r):
            cp.start()


    def to_core(d, carry):
        for p in range(3):
            x_copy(d, p).wait_recv()
        core_copy(d).start()
        return carry

    def attend_row(d):
        core_copy(d).wait_recv()
        attend(
            kvbuf[0, z - d].reshape(2 * TOK, HEAD_DIM), kvbuf[1, z - d].reshape(2 * TOK, HEAD_DIM),
            None, False,
        )

    def near_row(d, carry):
        attend_row(d)
        return carry

    def forward_far(d, carry):
        @pl.when((late == 0) | (d < 4) | (d > 4))
        def _():
            forward(d, 0)

        return carry

    lax.fori_loop(near, z + 1, forward_far, 0)
    lax.fori_loop(1, near, to_core, 0)
    core_copy_own().wait_recv()

    @pl.when(xh == 1)
    def _():
        attend(
            kvbuf[0, z, 0].reshape(TOK, HEAD_DIM), kvbuf[1, z, 0].reshape(TOK, HEAD_DIM),
            None, False,
        )

    lax.fori_loop(1, near, near_row, 0)


    def b_all():
        return remote(in_b, in_b, b_s, b_r, c, sib)

    b_all().wait_recv()
    entering = in_b[...].reshape(STATE, CHAN)
    squares = jnp.zeros((TOK, 128), F32)
    for part in range(2):
        cols = slice(part * 256, (part + 1) * 256)
        reach = jnp.dot(cb_v[...], entering[:, cols], preferred_element_type=F32)
        gated = (pre_v[:, cols] + ecx_v[:, cols] * reach) * sz_v[:, cols]
        pre_v[:, cols] = gated
        squares = squares + gated[:, :128] * gated[:, :128] + gated[:, 128:] * gated[:, 128:]
    sq_v[0] = jnp.sum(squares.T, axis=0, keepdims=True)

    def quad_copies():
        return [
            remote(sq_v.at[0], sq_v.at[1], q_s.at[0], q_r.at[0], c, sib),
            remote(sq_v.at[0], sq_v.at[2], q_s.at[1], q_r.at[1], c, hd + flip_l),
            remote(sq_v.at[0], sq_v.at[3], q_s.at[2], q_r.at[2], c, sib + flip_l),
        ]

    for cp in quad_copies():
        cp.start()

    def far_row(d, carry):
        to_core(d, 0)

        @pl.when(d > near)
        def _():
            attend_row(d - 1)

        return carry

    lax.fori_loop(near, z + 1, far_row, 0)

    for cp in quad_copies():
        cp.wait_recv()
    group_total = sq_v[0] + sq_v[1] + sq_v[2] + sq_v[3]
    scale = lax.rsqrt(group_total * (1.0 / 2048.0) + EPSILON)
    scale_col = jnp.broadcast_to(scale, (8, TOK)).T[:, 0:1]
    ssm_v[...] = (pre_v[...] * scale_col * gain_ref[...]).astype(BF16)
    ssm_out = pltpu.make_async_copy(ssm_v, ssm_hbm, loc.at[12])
    ssm_out.start()

    @pl.when(grp > 0)
    def _():
        attend_row(z)

    attn_out = []
    for h in range(2):
        mine = slice(h * TOK, (h + 1) * TOK)
        attn_v[h] = (o_v[:, mine] / l_v[:, mine]).T.astype(BF16)
        attn_out.append(
            pltpu.make_async_copy(
                attn_v.at[h], attn_hbm.at[:, pl.ds(h * HEAD_DIM, HEAD_DIM)], loc.at[13 + h]
            )
        )
        attn_out[h].start()

    @pl.when(c < N_CTX - 1)
    def _():
        for cp in halo_copies():
            cp.wait_send()

    def group_sent(size, each, mates):
        dec_all(size).wait_send()
        a_all().wait_send()
        b_all().wait_send()

    for_group(group_sent)

    @pl.when(grp == 0)
    def _():
        e_copy().wait_send()
        remote(e_out, e_in, f_s, f_r, c, sib).wait_send()

    @pl.when(grp == 1)
    def _():
        remote(e_out, e_in, t_s, t_r, c, sib).wait_send()
        two = pl.ds(0, 2)
        remote(dec_in.at[two], dec_in.at[two], lt_s, lt_r, c, sib).wait_send()

    def kv1_sent(d, carry):
        kv1_copy(d).wait_send()
        return carry

    lax.fori_loop(1, z_last + 1 - z, kv1_sent, 0)

    @pl.when(grp == 0)
    def _():
        for row in (2, 3):
            kv1_copy(row - z).wait_send()

    @pl.when(late == 0)
    def _():
        kv1_copy(4).wait_send()

    @pl.when(late == 1)
    def _():
        for e in range(1, 4):
            relay_copy(e).wait_send()

    def row_sent(d, carry):
        for p in range(3):
            x_copy(d, p).wait_send()
        core_copy(d).wait_send()
        return carry

    lax.fori_loop(1, z + 1, row_sent, 0)
    for p in (1, 2):
        x_copy(0, p).wait_send()
    core_copy_own().wait_send()
    for cp in quad_copies():
        cp.wait_send()
    ssm_out.wait()
    for cp in attn_out:
        cp.wait()


def hand_over(ssm_in, attn_in, ssm_ref, attn_ref, ssm_v, attn_v, sems):
    into = [
        pltpu.make_async_copy(ssm_in, ssm_v, sems.at[0]),
        pltpu.make_async_copy(attn_in, attn_v, sems.at[1]),
    ]
    out = [
        pltpu.make_async_copy(ssm_v, ssm_ref, sems.at[2]),
        pltpu.make_async_copy(attn_v, attn_ref, sems.at[3]),
    ]
    for cp in into:
        cp.start()
    for cp, later in zip(into, out):
        cp.wait()
        later.start()
    for cp in out:
        cp.wait()


def local(
    x_in, z_in, bc_in, dt_raw, a_log, d_skip, conv_x, conv_bc, norm_gain, queries, keys_values
):
    hbm = pl.BlockSpec(memory_space=pltpu.HBM)
    dma = pltpu.SemaphoreType.DMA
    out_shape = (
        jax.ShapeDtypeStruct((TOK, CHAN), BF16),
        jax.ShapeDtypeStruct((TOK, 2 * HEAD_DIM), BF16),
    )
    mixed = pl.pallas_call(
        kernel,
        out_shape=out_shape,
        in_specs=[hbm] * 11,
        out_specs=(hbm, hbm),
        scratch_shapes=[
            pltpu.VMEM((HEADS, TOK), F32),
            pltpu.SMEM((HEADS,), F32),
            pltpu.SMEM((HEADS,), F32),
            pltpu.VMEM((CONV, CHAN), BF16),
            pltpu.VMEM((CONV, 2 * GROUPS * STATE), BF16),
            pltpu.VMEM((1, CHAN), F32),
            pltpu.VMEM((TOK, CHAN), BF16),
            pltpu.VMEM((TOK, CHAN), BF16),
            pltpu.VMEM((TOK, STATE), BF16),
            pltpu.VMEM((TOK, STATE), BF16),
            pltpu.VMEM((TOK, 2 * HEAD_DIM), BF16),
            pltpu.VMEM((2 * TOK, HEAD_DIM), BF16),
            pltpu.VMEM((2, ROWS_Z, 2, 2, 2, QUART, HEAD_DIM), BF16),
            pltpu.VMEM((16, CHAN), BF16),
            pltpu.VMEM((2, 16, STATE), BF16),
            pltpu.VMEM((8 + TOK, CHAN), F32),
            pltpu.VMEM((8 + TOK, 2 * STATE), F32),
            pltpu.VMEM((TOK, STATE), F32),
            pltpu.VMEM((8, SLICE, CHAN), BF16),
            pltpu.VMEM((8, 2, SLICE, CHAN), BF16),
            pltpu.VMEM((8, 2, SLICE, CHAN), BF16),
            pltpu.VMEM((8, SLICE, CHAN), BF16),
            pltpu.VMEM((2, SLICE, CHAN), BF16),
            pltpu.VMEM((2, SLICE, CHAN), BF16),
            pltpu.VMEM((1, SLICE, CHAN), BF16),
            pltpu.VMEM((1, CHAN), F32),
            pltpu.VMEM((1, CHAN), F32),
            pltpu.VMEM((1, CHAN), F32),
            pltpu.VMEM((8, 1, CHAN), F32),
            pltpu.VMEM((TOK, CHAN), F32),
            pltpu.VMEM((TOK, CHAN), F32),
            pltpu.VMEM((TOK, CHAN), F32),
            pltpu.VMEM((TOK, STATE), BF16),
            pltpu.VMEM((4, 1, TOK), F32),
            pltpu.VMEM((1, 2 * TOK), F32),
            pltpu.VMEM((1, 2 * TOK), F32),
            pltpu.VMEM((HEAD_DIM, 2 * TOK), F32),
            pltpu.VMEM((TOK, CHAN), BF16),
            pltpu.VMEM((2, TOK, HEAD_DIM), BF16),
            dma((15,)), dma((3,)), dma((3,)),
            dma(()), dma(()), dma(()), dma(()), dma(()), dma(()), dma(()), dma(()),
            dma(()), dma(()), dma(()), dma(()), dma(()), dma(()),
            dma((3,)), dma((3,)), dma((ROWS_Z,)), dma((ROWS_Z,)),
            dma((ROWS_Z, 3)), dma((ROWS_Z, 3)), dma((ROWS_Z,)), dma((ROWS_Z,)),
            pltpu.SemaphoreType.REGULAR((2,)),
            pltpu.SemaphoreType.REGULAR, dma((4,)),
        ],
        compiler_params=pltpu.CompilerParams(
            collective_id=0, has_side_effects=True, vmem_limit_bytes=64 * 1024 * 1024
        ),
        name="mixer",
    )(
        x_in, z_in, bc_in, dt_raw, a_log, d_skip, conv_x, conv_bc,
        norm_gain.reshape(1, CHAN), queries,
        keys_values.reshape(2, 2, 2, QUART, GROUPS * HEAD_DIM),
    )
    return pl.pallas_call(
        hand_over,
        out_shape=out_shape,
        in_specs=[hbm, hbm],
        out_specs=(hbm, hbm),
        scratch_shapes=[
            pltpu.VMEM((TOK, CHAN), BF16), pltpu.VMEM((TOK, 2 * HEAD_DIM), BF16), dma((4,)),
        ],
        name="hand_over",
    )(*mixed)


def solution(mesh):
    placed = (
        P("ctx", "head"),
        P("ctx", "head"),
        P("ctx", None),
        P("head", "ctx"),
        P("head"),
        P("head"),
        P(None, "head"),
        P(),
        P("head"),
        P("ctx", "head"),
        P(None, "ctx", None),
    )
    return jax.shard_map(
        local,
        mesh=mesh,
        in_specs=placed,
        out_specs=(P("ctx", "head"), P("ctx", "head")),
        check_vma=False,
    )
```

```python
import functools
import math

import jax
import jax.numpy as jnp
from jax import lax
from jax.experimental import pallas as pl
from jax.experimental.pallas import tpu as pltpu
from jax.sharding import PartitionSpec as P

GROUPS = 8
STATE = 128
HEAD_DIM = 128
CONV = 4
TOK = 256
HEADS = 8
CHAN = 512
N_CTX = 16
BLOCK = 128
ROWS_Z = 8
SLICE = STATE // 8
QUART = TOK // 4
EPSILON = 1e-05
NEGATIVE = -1e30
HIGH = lax.Precision.HIGHEST
MESH = pl.DeviceIdType.MESH
F32 = jnp.float32
BF16 = jnp.bfloat16
PEERS = ((0, 1), (1, 0), (1, 1))
EXP_SCALE = math.log2(math.e) / math.sqrt(HEAD_DIM)


def silu(v):
    return v / (1.0 + jnp.exp(-v))


def conv_rows(pad_ref, taps, cols, rows):
    total = jnp.zeros((rows, cols.size), F32)
    for k in range(CONV):
        total = total + pad_ref[5 + k : 5 + k + rows, cols] * taps[k : k + 1]
    return silu(total)


def kernel(
    x_hbm, z_hbm, bc_hbm, dt_hbm, alog_hbm, dskip_hbm, cx_hbm, cbc_hbm, gain_hbm, q_hbm, kv_hbm,
    ssm_hbm, attn_hbm,
    dt_ref, alog_ref, dskip_ref, cx_ref, cbc_ref, gain_ref,
    x_v, z_v, b_v, c_v, q_v, q2_v, kvbuf, halo_x, halo_bc, pad_x, pad_bc, bf_v,
    st_send, in_a, out_b, in_b, e_out, e_in, t_in, lt_out, lt_in, dec_send, dec_in, pre_v, sz_v, ecx_v, cb_v, sq_v,
    m_v, l_v, o_v, ssm_v, attn_v,
    loc, h_s, h_r, d_s, d_r, a_s, a_r, b_s, b_r, e_s, e_r, f_s, f_r, t_s, t_r, lt_s, lt_r, q_s, q_r, s1_s, s1_r,
    x_s, x_r, c_s, c_r, rdy, rdy_e, r_s,
):
    c = lax.axis_index("ctx")
    hd = lax.axis_index("head")
    z, xh = lax.div(c, 2), lax.rem(c, 2)
    late = lax.div(c, 8)
    grp = lax.div(c, 4) - lax.div(c, 12)
    mem = (1 - late) * lax.rem(c, 4) + late * (c - 8)
    z_first = 2 * grp
    z_last = z_first + 1 + 2 * late
    y, qi = lax.div(hd, 4), lax.rem(hd, 4)
    xl, core = lax.div(qi, 2), lax.rem(qi, 2)
    flip_c = 1 - 2 * xh
    flip_l = 2 * (1 - 2 * xl)
    sib = hd + 1 - 2 * core
    hf = hd + flip_l
    ycol = pl.multiple_of(y * 128, 128)
    ycol2 = pl.multiple_of(GROUPS * STATE + y * 128, 128)

    def for_group(act):
        @pl.when(late == 0)
        def _():
            act(4, 2, [lax.rem(mem + e, 4) for e in range(1, 4)])

        @pl.when(late == 1)
        def _():
            act(8, 1, [lax.rem(mem + e, 8) for e in range(1, 8)])

    def remote(src, dst, ss, rs, ctx, head):
        return pltpu.make_async_remote_copy(
            src_ref=src, dst_ref=dst, send_sem=ss, recv_sem=rs,
            device_id=(ctx, head), device_id_type=MESH,
        )

    small = [
        pltpu.make_async_copy(src, dst, loc.at[i])
        for i, (src, dst) in enumerate(
            (
                (dt_hbm, dt_ref), (alog_hbm, alog_ref), (dskip_hbm, dskip_ref),
                (cx_hbm, cx_ref), (cbc_hbm, cbc_ref), (gain_hbm, gain_ref),
            )
        )
    ]
    load_x = pltpu.make_async_copy(x_hbm, x_v, loc.at[6])
    load_b = pltpu.make_async_copy(bc_hbm.at[:, pl.ds(ycol, 128)], b_v, loc.at[7])
    load_c = pltpu.make_async_copy(bc_hbm.at[:, pl.ds(ycol2, 128)], c_v, loc.at[8])
    load_q = pltpu.make_async_copy(q_hbm, q_v, loc.at[9])
    load_z = pltpu.make_async_copy(z_hbm, z_v, loc.at[10])
    load_kv = pltpu.make_async_copy(
        kv_hbm.at[:, :, :, :, pl.ds(ycol, 128)], kvbuf.at[:, z, xh], loc.at[11]
    )
    for cp in small + [load_b, load_c, load_x, load_kv, load_q, load_z]:
        cp.start()

    barrier = pltpu.get_barrier_semaphore()

    def greet(ctx, head):
        pl.semaphore_signal(barrier, inc=1, device_id=(ctx, head), device_id_type=MESH)

    def greet_mates(size, each, mates):
        for to in mates:
            greet(c - mem + to, hd)
            greet(c - mem + to, hf)

    for_group(greet_mates)
    greet(c, sib)
    greet(c, hd + flip_l)
    greet(c, sib + flip_l)
    greet(c + flip_c, hd + flip_l)

    @pl.when((mem == 0) & (c > 0))
    def _():
        greet(c - 1, hd)

    @pl.when(grp < 2)
    def _():
        for k in range(2):
            greet(8 + 2 * mem + k, hd)

    @pl.when(grp == 0)
    def _():
        for row in (2, 3):
            greet(2 * row + xh, hd)

    @pl.when(grp < 2)
    def _():
        greet(c + 8, hd)

    for cp in small:
        cp.wait()
    a_log = jnp.zeros((HEADS, 1), F32)
    head_row = lax.broadcasted_iota(jnp.int32, (HEADS, 1), 0)
    for h in range(HEADS):
        a_log = jnp.where(head_row == h, alog_ref[h], a_log)
    step = jnp.log(1.0 + jnp.exp(dt_ref[...]))
    cum = -jnp.exp(a_log) * step
    lane = lax.broadcasted_iota(jnp.int32, (HEADS, TOK), 1)
    shift = 1
    while shift < TOK:
        cum = cum + jnp.where(lane >= shift, pltpu.roll(cum, shift, 1), 0.0)
        shift *= 2
    last = cum[:, TOK - 1 : TOK]
    of_head = (
        lax.div(lax.broadcasted_iota(jnp.int32, (HEADS, CHAN), 1), CHAN // HEADS)
        == lax.broadcasted_iota(jnp.int32, (HEADS, CHAN), 0)
    )
    spread = jnp.where(of_head, 1.0, 0.0).astype(F32)
    dec_send[...] = jnp.sum(jnp.where(of_head, last, 0.0), axis=0, keepdims=True)
    tail = jnp.exp(last - cum) * step
    tail_x = jnp.dot(tail.T, spread, precision=HIGH, preferred_element_type=F32)

    greeted = 2 * (3 + 4 * late) + 4 + jnp.where(grp == 1, 2, 0) + 3 * late + jnp.where((mem == 3) & (late == 0), 1, 0)
    pl.semaphore_wait(barrier, greeted)

    def halo_copies():
        tail_rows = pl.ds(TOK - 16, 16)
        return [
            remote(x_hbm.at[tail_rows, :], halo_x, h_s.at[0], h_r.at[0], c + 1, hd),
            remote(
                bc_hbm.at[tail_rows, pl.ds(ycol, 128)], halo_bc.at[0],
                h_s.at[1], h_r.at[1], c + 1, hd,
            ),
            remote(
                bc_hbm.at[tail_rows, pl.ds(ycol2, 128)], halo_bc.at[1],
                h_s.at[2], h_r.at[2], c + 1, hd,
            ),
        ]

    @pl.when(c < N_CTX - 1)
    def _():
        for cp in halo_copies():
            cp.start()

    def say_ready(sem, ctx):
        pl.semaphore_signal(sem, inc=1, device_id=(ctx, hd), device_id_type=MESH)

    @pl.when(grp == 1)
    def _():
        for row in range(2):
            say_ready(rdy.at[0], 2 * row + xh)

    @pl.when(grp == 2)
    def _():
        say_ready(rdy.at[1], c - 8)
        say_ready(rdy_e, lax.div(mem, 2))
        say_ready(rdy_e, 4 + lax.div(mem, 2))

    def dec_copy(to):
        return remote(dec_send, dec_in.at[mem], d_s, d_r, c - mem + to, hf)

    def dec_start(size, each, mates):
        for to in mates + [mem]:
            dec_copy(to).start()

    for_group(dec_start)

    def kv1_copy(d):
        return remote(
            kvbuf.at[:, z, xh, xl, core], kvbuf.at[:, z, xh, xl, core],
            s1_s.at[d], s1_r.at[d], c + 2 * d, hd,
        )

    def kv1_got(d):
        piece = kvbuf.at[:, z - d, xh, xl, core]
        return remote(piece, piece, s1_s.at[d], s1_r.at[d], c, sib)

    def kv1_start(d, carry):
        kv1_copy(d).start()
        return carry

    def kv1_next():
        pl.semaphore_wait(rdy.at[0], 2)
        for row in (2, 3):
            kv1_copy(row - z).start()

    def kv1_late():
        pl.semaphore_wait(rdy.at[1], 1)
        kv1_copy(4).start()

    def relay_copy(e):
        row = 4 + lax.rem(z - 4 + e, 4)
        piece = kvbuf.at[:, z - 4, xh, xl, core]
        return remote(piece, piece, r_s.at[e], s1_r.at[row + 4 - z], 2 * row + xh, hd)

    def x_copy(d, p):
        fh, fl = PEERS[p]
        piece = kvbuf.at[:, z - d, xh, xl, core]
        return remote(piece, piece, x_s.at[d, p], x_r.at[d, p], c + fh * flip_c, hd + fl * flip_l)

    def core_copy(d):
        piece = kvbuf.at[:, z - d, :, :, core]
        return remote(piece, piece, c_s.at[d], c_r.at[d], c, sib)

    def core_copy_own():
        piece = kvbuf.at[:, z, 1 - xh, :, core]
        return remote(piece, piece, c_s.at[0], c_r.at[0], c, sib)

    load_kv.wait()
    for p in (1, 2):
        x_copy(0, p).start()
    lax.fori_loop(1, z_last + 1 - z, kv1_start, 0)

    taps_b = cbc_ref[:, pl.ds(ycol, 128)].astype(F32)
    taps_c = cbc_ref[:, pl.ds(ycol2, 128)].astype(F32)
    taps_x = cx_ref[...].astype(F32)
    pad_bc[0:8] = jnp.zeros((8, 2 * STATE), F32)
    pad_x[0:8] = jnp.zeros((8, CHAN), F32)
    load_b.wait()
    load_c.wait()
    pad_bc[8:, 0:STATE] = b_v[...].astype(F32)
    pad_bc[8:, STATE:] = c_v[...].astype(F32)

    def convolve(rows):
        bf_v[0:rows] = conv_rows(pad_bc, taps_b, pl.ds(0, STATE), rows)
        cb_v[0:rows] = conv_rows(pad_bc, taps_c, pl.ds(STATE, STATE), rows).astype(BF16)
        x_v[0:rows] = conv_rows(pad_x, taps_x, pl.ds(0, CHAN), rows).astype(BF16)

    load_x.wait()
    pad_x[8:] = x_v[...].astype(F32)
    convolve(TOK)

    def attend(keys, values, mask, first):
        logits = lax.dot_general(
            keys, q2_v[...], (((1,), (1,)), ((), ())), preferred_element_type=F32
        )
        if mask is not None:
            logits = jnp.where(mask, logits, NEGATIVE)
        top = jnp.max(logits, axis=0, keepdims=True)
        if not first:
            top = jnp.maximum(m_v[...], top)
        grown = jnp.exp2((logits - top) * EXP_SCALE)
        if mask is not None:
            grown = jnp.where(mask, grown, 0.0)
        den = jnp.sum(grown, axis=0, keepdims=True)
        got = jnp.dot(values.T, grown.astype(BF16), preferred_element_type=F32)
        if first:
            l_v[...] = den
            o_v[...] = got
        else:
            shrink = jnp.exp2((m_v[...] - top) * EXP_SCALE)
            l_v[...] = l_v[...] * shrink + den
            o_v[...] = o_v[...] * shrink + got
        m_v[...] = top

    load_q.wait()
    q2_v[0:TOK] = q_v[:, :HEAD_DIM]
    q2_v[TOK:] = q_v[:, HEAD_DIM:]
    key_at = lax.broadcasted_iota(jnp.int32, (TOK, 2 * TOK), 0)
    query_at = lax.rem(lax.broadcasted_iota(jnp.int32, (TOK, 2 * TOK), 1), TOK)
    attend(
        kvbuf[0, z, xh].reshape(TOK, HEAD_DIM), kvbuf[1, z, xh].reshape(TOK, HEAD_DIM),
        key_at <= query_at, True,
    )
    @pl.when(c > 0)
    def _():
        for cp in halo_copies():
            cp.wait_recv()
        pad_bc[0:8, 0:STATE] = halo_bc[0].astype(F32)[8:16]
        pad_bc[0:8, STATE:] = halo_bc[1].astype(F32)[8:16]
        pad_x[0:8] = halo_x[...].astype(F32)[8:16]
        convolve(16)

    b_t = bf_v[...].T.astype(BF16)
    carried = (tail_x * x_v[...].astype(F32)).astype(BF16)
    state = jnp.dot(b_t, carried, preferred_element_type=F32).astype(BF16)
    st_send[...] = state.reshape(8, SLICE, CHAN)

    def a_start(size, each, mates):
        for to in mates + [mem]:
            remote(
                st_send.at[pl.ds(each * to, each)], in_a.at[mem, pl.ds(0, each)],
                a_s, a_r, c - mem + to, hf,
            ).start()

    def a_all():
        return remote(st_send, st_send, a_s, a_r, c, sib)

    for_group(a_start)

    @pl.when(grp == 0)
    def _():
        kv1_next()


    scores = jnp.dot(cb_v[...], b_t, preferred_element_type=F32)
    t_at = lax.broadcasted_iota(jnp.int32, (TOK, TOK), 0)
    s_at = lax.broadcasted_iota(jnp.int32, (TOK, TOK), 1)
    scores = jnp.where(s_at <= t_at, scores, 0.0)
    cum_t = cum.T
    skip_row = jnp.zeros((1, CHAN), F32)
    head_of_lane = lax.div(lax.broadcasted_iota(jnp.int32, (1, CHAN), 1), CHAN // HEADS)
    for h in range(HEADS):
        skip_row = jnp.where(head_of_lane == h, dskip_ref[h], skip_row)
    left = lax.broadcasted_iota(jnp.int32, (BLOCK, 128), 1) < 64
    for low in (0, BLOCK):
        rows, upto = slice(low, low + BLOCK), low + BLOCK
        for pair in range(HEADS // 2):
            cols = slice(128 * pair, 128 * pair + 128)
            both = []
            for h in (2 * pair, 2 * pair + 1):
                gap = jnp.minimum(cum_t[rows, h : h + 1] - cum[h : h + 1, :upto], 0.0)
                weights = (scores[rows, :upto] * jnp.exp(gap) * step[h : h + 1, :upto]).astype(BF16)
                both.append(jnp.dot(weights, x_v[:upto, cols], preferred_element_type=F32))
            pre_v[rows, cols] = (
                jnp.where(left, both[0], both[1])
                + skip_row[:, cols] * x_v[rows, cols].astype(F32)
            )
    ecx_v[...] = jnp.dot(jnp.exp(cum).T, spread, precision=HIGH, preferred_element_type=F32)
    load_z.wait()
    sz_v[...] = silu(z_v[...].astype(F32))

    @pl.when(grp == 1)
    def _():
        kv1_late()

    for p in (1, 2):
        x_copy(0, p).wait_recv()
    core_copy_own().start()

    def forward(d, carry):
        kv1_got(d).wait_recv()
        for p in (1, 0, 2):
            x_copy(d, p).start()
        return carry

    near = z - z_first + 1
    lax.fori_loop(1, near, forward, 0)

    @pl.when(late == 1)
    def _():
        kv1_got(4).wait_recv()
        for e in range(1, 4):
            relay_copy(e).start()
        for p in range(3):
            x_copy(4, p).start()

    def dec_all(size):
        some = pl.ds(0, size)
        return remote(dec_in.at[some], dec_in.at[some], d_s, d_r, c, sib)

    one = pl.ds(0, 1)

    def e_copy():
        return remote(e_out, e_in, e_s, e_r, c + 4, hd)

    def to_late(src, dst, sem, got):
        return [remote(src(k), dst, sem, got, 8 + 2 * mem + k, hd) for k in range(2)]

    def scan(size, each, mates):
        dec_all(size).wait_recv()
        a_all().wait_recv()
        part = pl.ds(0, each)

        def steps(state, keep):
            for k in range(size):
                if keep:
                    out_b[k, 0:each] = state.astype(BF16)
                state = jnp.exp(dec_in[k]) * state + in_a[k, 0:each].astype(F32)
            return state

        if size == 8:
            remote(e_in.at[one], e_in.at[one], f_s, f_r, c, sib).wait_recv()
            remote(t_in, t_in, t_s, t_r, c, sib).wait_recv()
            remote(lt_in, lt_in, lt_s, lt_r, c, sib).wait_recv()
            start = jnp.exp(lt_in[...]) * e_in[0:1].astype(F32) + t_in[...].astype(F32)
            steps(start, True)
        else:
            e_out[...] = steps(jnp.zeros((each, SLICE, CHAN), F32), True).astype(BF16)

            @pl.when(grp == 0)
            def _():
                e_copy().start()
                kv1_late()

            @pl.when(grp == 1)
            def _():
                lt_out[...] = dec_in[0] + dec_in[1] + dec_in[2] + dec_in[3]
                pl.semaphore_wait(rdy_e, 2)
                for cp in to_late(lambda k: e_out.at[pl.ds(k, 1)], t_in, t_s, t_r):
                    cp.start()
                for cp in to_late(lambda k: lt_out, lt_in, lt_s, lt_r):
                    cp.start()
                remote(e_in, e_in, e_s, e_r, c, sib).wait_recv()
                steps(e_in[...].astype(F32), True)

        for to in mates + [mem]:
            remote(
                out_b.at[to, part], in_b.at[pl.ds(each * mem, each)],
                b_s, b_r, c - mem + to, hf,
            ).start()

    for_group(scan)

    @pl.when(grp == 0)
    def _():
        pl.semaphore_wait(rdy_e, 2)
        for cp in to_late(lambda k: e_out.at[pl.ds(k, 1)], e_in.at[one], f_s, f_r):
            cp.start()


    def to_core(d, carry):
        for p in range(3):
            x_copy(d, p).wait_recv()
        core_copy(d).start()
        return carry

    def attend_row(d):
        core_copy(d).wait_recv()
        attend(
            kvbuf[0, z - d].reshape(2 * TOK, HEAD_DIM), kvbuf[1, z - d].reshape(2 * TOK, HEAD_DIM),
            None, False,
        )

    def near_row(d, carry):
        attend_row(d)
        return carry

    def forward_far(d, carry):
        @pl.when((late == 0) | (d < 4) | (d > 4))
        def _():
            forward(d, 0)

        return carry

    lax.fori_loop(near, z + 1, forward_far, 0)
    lax.fori_loop(1, near, to_core, 0)
    core_copy_own().wait_recv()

    @pl.when(xh == 1)
    def _():
        attend(
            kvbuf[0, z, 0].reshape(TOK, HEAD_DIM), kvbuf[1, z, 0].reshape(TOK, HEAD_DIM),
            None, False,
        )

    lax.fori_loop(1, near, near_row, 0)


    def b_all():
        return remote(in_b, in_b, b_s, b_r, c, sib)

    b_all().wait_recv()
    entering = in_b[...].reshape(STATE, CHAN)
    squares = jnp.zeros((TOK, 128), F32)
    for part in range(2):
        cols = slice(part * 256, (part + 1) * 256)
        reach = jnp.dot(cb_v[...], entering[:, cols], preferred_element_type=F32)
        gated = (pre_v[:, cols] + ecx_v[:, cols] * reach) * sz_v[:, cols]
        pre_v[:, cols] = gated
        squares = squares + gated[:, :128] * gated[:, :128] + gated[:, 128:] * gated[:, 128:]
    sq_v[0] = jnp.sum(squares.T, axis=0, keepdims=True)

    def quad_copies():
        return [
            remote(sq_v.at[0], sq_v.at[3], q_s.at[2], q_r.at[2], c, sib + flip_l),
            remote(sq_v.at[0], sq_v.at[2], q_s.at[1], q_r.at[1], c, hd + flip_l),
            remote(sq_v.at[0], sq_v.at[1], q_s.at[0], q_r.at[0], c, sib),
        ]

    for cp in quad_copies():
        cp.start()

    def far_row(d, carry):
        to_core(d, 0)

        @pl.when(d > near)
        def _():
            attend_row(d - 1)

        return carry

    lax.fori_loop(near, z + 1, far_row, 0)

    for cp in quad_copies():
        cp.wait_recv()
    group_total = sq_v[0] + sq_v[1] + sq_v[2] + sq_v[3]
    scale = lax.rsqrt(group_total * (1.0 / 2048.0) + EPSILON)
    scale_col = jnp.broadcast_to(scale, (8, TOK)).T[:, 0:1]
    ssm_v[...] = (pre_v[...] * scale_col * gain_ref[...]).astype(BF16)
    ssm_out = pltpu.make_async_copy(ssm_v, ssm_hbm, loc.at[12])
    ssm_out.start()

    @pl.when(grp > 0)
    def _():
        attend_row(z)

    result = o_v[...] / l_v[...]
    for h in range(2):
        attn_v[:, h * HEAD_DIM : (h + 1) * HEAD_DIM] = result[
            :, h * TOK : (h + 1) * TOK
        ].T.astype(BF16)
    attn_out = pltpu.make_async_copy(attn_v, attn_hbm, loc.at[13])
    attn_out.start()

    @pl.when(c < N_CTX - 1)
    def _():
        for cp in halo_copies():
            cp.wait_send()

    def group_sent(size, each, mates):
        dec_all(size).wait_send()
        a_all().wait_send()
        b_all().wait_send()

    for_group(group_sent)

    @pl.when(grp == 0)
    def _():
        e_copy().wait_send()
        remote(e_out, e_in, f_s, f_r, c, sib).wait_send()

    @pl.when(grp == 1)
    def _():
        remote(e_out, e_in, t_s, t_r, c, sib).wait_send()
        two = pl.ds(0, 2)
        remote(dec_in.at[two], dec_in.at[two], lt_s, lt_r, c, sib).wait_send()

    def kv1_sent(d, carry):
        kv1_copy(d).wait_send()
        return carry

    lax.fori_loop(1, z_last + 1 - z, kv1_sent, 0)

    @pl.when(grp == 0)
    def _():
        for row in (2, 3):
            kv1_copy(row - z).wait_send()

    @pl.when(late == 0)
    def _():
        kv1_copy(4).wait_send()

    @pl.when(late == 1)
    def _():
        for e in range(1, 4):
            relay_copy(e).wait_send()

    def row_sent(d, carry):
        for p in range(3):
            x_copy(d, p).wait_send()
        core_copy(d).wait_send()
        return carry

    lax.fori_loop(1, z + 1, row_sent, 0)
    for p in (1, 2):
        x_copy(0, p).wait_send()
    core_copy_own().wait_send()
    for cp in quad_copies():
        cp.wait_send()
    ssm_out.wait()
    attn_out.wait()


def hand_over(ssm_in, attn_in, ssm_ref, attn_ref, ssm_v, attn_v, sems):
    into = [
        pltpu.make_async_copy(ssm_in, ssm_v, sems.at[0]),
        pltpu.make_async_copy(attn_in, attn_v, sems.at[1]),
    ]
    out = [
        pltpu.make_async_copy(ssm_v, ssm_ref, sems.at[2]),
        pltpu.make_async_copy(attn_v, attn_ref, sems.at[3]),
    ]
    for cp in into:
        cp.start()
    for cp, later in zip(into, out):
        cp.wait()
        later.start()
    for cp in out:
        cp.wait()


def local(
    x_in, z_in, bc_in, dt_raw, a_log, d_skip, conv_x, conv_bc, norm_gain, queries, keys_values
):
    hbm = pl.BlockSpec(memory_space=pltpu.HBM)
    dma = pltpu.SemaphoreType.DMA
    out_shape = (
        jax.ShapeDtypeStruct((TOK, CHAN), BF16),
        jax.ShapeDtypeStruct((TOK, 2 * HEAD_DIM), BF16),
    )
    mixed = pl.pallas_call(
        kernel,
        out_shape=out_shape,
        in_specs=[hbm] * 11,
        out_specs=(hbm, hbm),
        scratch_shapes=[
            pltpu.VMEM((HEADS, TOK), F32),
            pltpu.SMEM((HEADS,), F32),
            pltpu.SMEM((HEADS,), F32),
            pltpu.VMEM((CONV, CHAN), BF16),
            pltpu.VMEM((CONV, 2 * GROUPS * STATE), BF16),
            pltpu.VMEM((1, CHAN), F32),
            pltpu.VMEM((TOK, CHAN), BF16),
            pltpu.VMEM((TOK, CHAN), BF16),
            pltpu.VMEM((TOK, STATE), BF16),
            pltpu.VMEM((TOK, STATE), BF16),
            pltpu.VMEM((TOK, 2 * HEAD_DIM), BF16),
            pltpu.VMEM((2 * TOK, HEAD_DIM), BF16),
            pltpu.VMEM((2, ROWS_Z, 2, 2, 2, QUART, HEAD_DIM), BF16),
            pltpu.VMEM((16, CHAN), BF16),
            pltpu.VMEM((2, 16, STATE), BF16),
            pltpu.VMEM((8 + TOK, CHAN), F32),
            pltpu.VMEM((8 + TOK, 2 * STATE), F32),
            pltpu.VMEM((TOK, STATE), F32),
            pltpu.VMEM((8, SLICE, CHAN), BF16),
            pltpu.VMEM((8, 2, SLICE, CHAN), BF16),
            pltpu.VMEM((8, 2, SLICE, CHAN), BF16),
            pltpu.VMEM((8, SLICE, CHAN), BF16),
            pltpu.VMEM((2, SLICE, CHAN), BF16),
            pltpu.VMEM((2, SLICE, CHAN), BF16),
            pltpu.VMEM((1, SLICE, CHAN), BF16),
            pltpu.VMEM((1, CHAN), F32),
            pltpu.VMEM((1, CHAN), F32),
            pltpu.VMEM((1, CHAN), F32),
            pltpu.VMEM((8, 1, CHAN), F32),
            pltpu.VMEM((TOK, CHAN), F32),
            pltpu.VMEM((TOK, CHAN), F32),
            pltpu.VMEM((TOK, CHAN), F32),
            pltpu.VMEM((TOK, STATE), BF16),
            pltpu.VMEM((4, 1, TOK), F32),
            pltpu.VMEM((1, 2 * TOK), F32),
            pltpu.VMEM((1, 2 * TOK), F32),
            pltpu.VMEM((HEAD_DIM, 2 * TOK), F32),
            pltpu.VMEM((TOK, CHAN), BF16),
            pltpu.VMEM((TOK, 2 * HEAD_DIM), BF16),
            dma((14,)), dma((3,)), dma((3,)),
            dma(()), dma(()), dma(()), dma(()), dma(()), dma(()), dma(()), dma(()),
            dma(()), dma(()), dma(()), dma(()), dma(()), dma(()),
            dma((3,)), dma((3,)), dma((ROWS_Z,)), dma((ROWS_Z,)),
            dma((ROWS_Z, 3)), dma((ROWS_Z, 3)), dma((ROWS_Z,)), dma((ROWS_Z,)),
            pltpu.SemaphoreType.REGULAR((2,)),
            pltpu.SemaphoreType.REGULAR, dma((4,)),
        ],
        compiler_params=pltpu.CompilerParams(
            collective_id=0, has_side_effects=True, vmem_limit_bytes=64 * 1024 * 1024
        ),
        name="mixer",
    )(
        x_in, z_in, bc_in, dt_raw, a_log, d_skip, conv_x, conv_bc,
        norm_gain.reshape(1, CHAN), queries,
        keys_values.reshape(2, 2, 2, QUART, GROUPS * HEAD_DIM),
    )
    return pl.pallas_call(
        hand_over,
        out_shape=out_shape,
        in_specs=[hbm, hbm],
        out_specs=(hbm, hbm),
        scratch_shapes=[
            pltpu.VMEM((TOK, CHAN), BF16), pltpu.VMEM((TOK, 2 * HEAD_DIM), BF16), dma((4,)),
        ],
        name="hand_over",
    )(*mixed)


def solution(mesh):
    placed = (
        P("ctx", "head"),
        P("ctx", "head"),
        P("ctx", None),
        P("head", "ctx"),
        P("head"),
        P("head"),
        P(None, "head"),
        P(),
        P("head"),
        P("ctx", "head"),
        P(None, "ctx", None),
    )
    return jax.shard_map(
        local,
        mesh=mesh,
        in_specs=placed,
        out_specs=(P("ctx", "head"), P("ctx", "head")),
        check_vma=False,
    )
```
